32 devices in a mesh: ens: 4 (over x, core), space: 8 (over z, y).
Axes of the slice: x: 2, y: 2, z: 4, core: 2. Of those that a mesh axis runs over, the one named last changes fastest.
Arguments:
- latents: bfloat16 [8, 32, 256, 256], P('ens', None, 'space'), may hold values from -6 to 6
- targets: bfloat16 [32, 256, 256], P(None, 'space'), may hold values from -6 to 6
- kernel: bfloat16 [3, 3, 256, 256], replicated, may hold values from -0.125 to 0.125
Outputs:
- loss: float32 [], replicated
- grad_input: bfloat16 [8, 32, 256, 256], P('ens', None, 'space')
- grad_kernel: float32 [3, 3, 256, 256], replicated
The draws below stay inside these ranges and needn't reach their ends.
All inputs are finite; a program needn't handle non-finite values.
Results may differ from the reference program's by a relative error of at most 0.0047.
Values may be sent and summed in bfloat16 or wider, within the bound.
A program may use at most 64 MiB of HBM per device.

```python
import jax
import jax.numpy as jnp
from jax import lax

C = 256
MEMBERS = 8
ROWS = 32
LON = 256


def level_of(stream_key, extent, split, smallest, high):
    factor_of = 1.0
    for position, blocks in split:
        steps = jax.random.uniform(jax.random.fold_in(jax.random.fold_in(stream_key, 6), position), (blocks,), jnp.float32, smallest / len(split), high / len(split))
        factor_of = factor_of * jnp.repeat(jnp.exp(steps), extent[position] // blocks).reshape((-1,) + (1,) * (len(extent) - 1 - position))
    return factor_of


def gaussian(rng, shape, scale, reach, shards=(), kind=jnp.bfloat16):
    result = jax.random.normal(rng, shape, jnp.float32) * scale
    if len(shards) > 0:
        result = level_of(rng, shape, shards, -0.22, 0.18) * result
    return jnp.clip(result, min=-reach, max=reach).astype(kind)


def setup_inputs(seed: int = 0) -> dict:
    key_of = jax.random.split(jax.random.key(seed), 4)
    latents = gaussian(key_of[0], (MEMBERS, ROWS, LON, C), 1.0, 6.0, ((0, 4), (2, 8)))
    targets = gaussian(key_of[1], (ROWS, LON, C), 1.0, 6.0, ((1, 8),))
    kernel = gaussian(key_of[2], (3, 3, C, C), (9 * C) ** -0.5, 0.125)
    return dict(latents=latents, targets=targets, kernel=kernel)


smoothing = 0.1

def border(field):
    wrapped = jnp.concatenate([field[:, :, -1:], field, field[:, :, :1]], axis=2)
    return jnp.pad(wrapped, ((0, 0), (1, 1), (0, 0), (0, 0)))

def conv_forward(padded, kernel, rows, cols):
    chans = padded.shape[3]
    total = None
    for row_off in range(3):
        for col_off in range(3):
            window = padded[:, row_off:row_off + rows, col_off:col_off + cols, :].reshape(-1, chans)
            term = jnp.dot(window, kernel[row_off, col_off], preferred_element_type=jnp.float32)
            total = term if total is None else total + term
    return total.reshape(padded.shape[0], rows, cols, -1)

def conv_adjoint(padded, kernel, rows, cols):
    chans = padded.shape[3]
    total = None
    for row_off in range(3):
        for col_off in range(3):
            window = padded[:, 2 - row_off:2 - row_off + rows, 2 - col_off:2 - col_off + cols, :].reshape(-1, chans)
            term = lax.dot_general(window, kernel[row_off, col_off], (((1,), (1,)), ((), ())), preferred_element_type=jnp.float32)
            total = term if total is None else total + term
    return total.reshape(padded.shape[0], rows, cols, -1)

def kernel_terms(padded, slopes, rows, cols):
    chans = padded.shape[3]
    flat_slopes = slopes.reshape(-1, slopes.shape[3])
    blocks = []
    for row_off in range(3):
        for col_off in range(3):
            window = padded[:, row_off:row_off + rows, col_off:col_off + cols, :].reshape(-1, chans)
            blocks.append(lax.dot_general(window, flat_slopes, (((0,), (0,)), ((), ())), preferred_element_type=jnp.float32))
    return jnp.stack(blocks).reshape(3, 3, chans, -1)

def reference(latents, targets, kernel):
    members, rows, cols, chans = latents.shape
    padded = border(latents)
    fields = conv_forward(padded, kernel, rows, cols)
    offset = fields - targets.astype(jnp.float32)[None]
    spread = jnp.sqrt(offset * offset + smoothing * smoothing)
    own_total = jnp.sum(spread)
    own_slope = offset / spread
    pair_total = jnp.zeros((), jnp.float32)
    slope_rows = []
    for member in range(members):
        accum = jnp.zeros(fields.shape[1:], jnp.float32)
        for other in range(members):
            if other != member:
                gap = fields[member] - fields[other]
                width = jnp.sqrt(gap * gap + smoothing * smoothing)
                pair_total = pair_total + jnp.sum(width)
                accum = accum + gap / width
        slope_rows.append(accum)
    pair_slope = jnp.stack(slope_rows)
    total = own_total / members - pair_total / (2 * members * (members - 1))
    loss = total / (rows * cols * chans)
    slopes = (own_slope / members - pair_slope / (members * (members - 1))).astype(jnp.bfloat16)
    grad_input = conv_adjoint(border(slopes), kernel, rows, cols).astype(jnp.bfloat16)
    grad_kernel = kernel_terms(padded, slopes, rows, cols) / (members * rows * cols)
    return (loss, grad_input, grad_kernel)
```

```python
import functools

import jax
import jax.numpy as jnp
from jax import lax
from jax.experimental import pallas as pl
from jax.experimental.pallas import tpu as pltpu
from jax.sharding import PartitionSpec as P

smoothing = 0.1
F32, BF16 = jnp.float32, jnp.bfloat16
NT = (((1,), (1,)), ((), ()))
TAPS = 9
BLOCKS = ((0, 4), (4, 8))


def pieces_of(n):
    units = -(-TAPS * 128 // (16 * n))
    pieces = min(3, units)
    return pieces, 16 * -(-units // pieces)


def body(
    n, members,
    lat_hbm, t_hbm, k_hbm,
    gi_ref, gk_ref, loss_ref,
    x_ref, latv, tv, kv, lef32, leo, lei, lef, fld, sp, acc, eo, ei, eh, gib, lacc,
    r1, g, b2, r2, b3, r3, b4, r4, l1, lr1, l2, lr2, l3, lr3,
    s_in, s_own, s_x, r_x, s_f, r_f, s_le, r_le, s_e, r_e, s_h, r_h, s_g, r_g,
    s_c, r_c, s_y, r_y, s_z, r_z, s_v, r_v, s_az, r_az, s_ay, r_ay, s_ac, r_ac,
    s_ls, r_ls, s_lp, r_lp,
):
    mdev, rows, cols, chans = lat_hbm.shape
    own = rows // 4
    last = own + 1
    cells = members * cols
    pieces, part = pieces_of(n)
    nz = n // 2
    half = part * nz
    span = 2 * half
    e = lax.axis_index("ens")
    s = lax.axis_index("space")
    core = lax.rem(e, 2)
    xx = e // 2
    sy = lax.rem(s, 2)
    sz = s // 2
    outer = xx != core
    cpeer = {"ens": xx * 2 + (1 - core)}
    xpeer = {"ens": (1 - xx) * 2 + core}
    across = {"ens": 3 - e}
    ypeer = {"space": sz * 2 + (1 - sy)}
    right_s = lax.rem(s + 1, n)
    left_s = lax.rem(s + n - 1, n)
    MESH = pl.DeviceIdType.MESH

    def rcopy(src, dst, ss, rs, dev):
        return pltpu.make_async_remote_copy(
            src_ref=src, dst_ref=dst, send_sem=ss, recv_sem=rs,
            device_id=dev, device_id_type=MESH,
        )

    def ens_at(d):
        return lax.rem(e + d, 4)

    def slot_of(c, q):
        return jnp.where(c == 0, last - q, q)

    def base_of(pair):
        return jnp.where(core == 0, own - 2 - 2 * pair, 2 * pair)

    in_lat = pltpu.make_async_copy(lat_hbm, latv, s_in.at[0])
    in_k = pltpu.make_async_copy(k_hbm, kv, s_in.at[1])
    in_t = pltpu.make_async_copy(t_hbm.at[pl.ds(e * own, own)], tv, s_in.at[2])
    in_lat.start()
    in_k.start()
    in_t.start()
    barrier = pltpu.get_barrier_semaphore()
    for d in range(1, 4):
        for strip in (s, right_s, left_s):
            pl.semaphore_signal(
                barrier, inc=1, device_id={"ens": ens_at(d), "space": strip}, device_id_type=MESH
            )

    @pl.loop(1, n)
    def _(d):
        pl.semaphore_signal(
            barrier, inc=1, device_id={"space": lax.rem(s + d, n)}, device_id_type=MESH
        )

    def own_copy(k):
        if k < mdev:
            return pltpu.make_async_copy(
                lat_hbm.at[k, pl.ds(e * own, own)], x_ref.at[1, pl.ds(1, own), e * mdev + k],
                s_own.at[k],
            )
        slot = slot_of(core, 0 if k == mdev else last)
        row = jnp.clip(e * own - 1 + slot, 0, rows - 1)
        return pltpu.make_async_copy(
            lat_hbm.at[:, row], x_ref.at[1, slot, pl.ds(e * mdev, mdev)], s_own.at[k]
        )

    for k in range(mdev + 1):
        own_copy(k).start()

    @pl.when(outer)
    def _():
        own_copy(mdev + 1).start()

    @pl.when(jnp.logical_not(outer))
    def _():
        blank = jnp.zeros((members, cols, chans), BF16)
        slot = slot_of(core, last)
        x_ref[1, slot] = blank
        for c in range(3):
            sp[c, slot] = blank

    lef32[...] = jnp.zeros_like(lef32)
    in_lat.wait()

    @pl.loop(0, rows)
    def _(row):
        for m in range(mdev):
            v = latv[m, row, 0:16].astype(F32)
            w = latv[m, row, cols - 16 : cols].astype(F32)
            lef32[0, pl.ds((1 + row) * mdev + m, 1)] = v[0:1]
            lef32[1, pl.ds((1 + row) * mdev + m, 1)] = w[15:16]

    leo[...] = lef32[...].astype(BF16)
    pl.semaphore_wait(barrier, n - 1 + 9)

    def row_of(d, to, q, src):
        slot = slot_of(lax.rem(to, 2), q)
        row = jnp.clip(to * own - 1 + slot, 0, rows - 1)
        return rcopy(
            lat_hbm.at[:, row], x_ref.at[1, slot, pl.ds(mdev * src, mdev)],
            s_x.at[d, q], r_x.at[src, q], {"ens": to},
        )

    def goes(to, q):
        there = (to // 2) != xx
        exists = (q < last) | ((to // 2) != lax.rem(to, 2))
        return exists & ((q > 0) | jnp.logical_not(there))

    def edge_of(side, d, src):
        to = ens_at(d)
        return rcopy(
            leo.at[side, pl.ds(pl.multiple_of(to * own * mdev, 16), 32)], lei.at[1 - side, src],
            s_le.at[side, d], r_le.at[1 - side, src],
            {"ens": to, "space": left_s if side == 0 else right_s},
        )

    @pl.loop(0, last + 1)
    def _(j):
        q = jnp.where(j < 3, lax.rem(j + 1, 3), j)
        for d in (2, 3, 1):
            to = ens_at(d)

            @pl.when(goes(to, q))
            def _():
                row_of(d, to, q, e).start()

        @pl.when(j == 1)
        def _():
            for d in (2, 3, 1, 0):
                for side in range(2):
                    edge_of(side, d, e).start()

    hand_slot = slot_of(core, 1)
    get_slot = slot_of(core, 0)
    theirs = pl.ds(2 * mdev * (1 - xx), 2 * mdev)
    hand = rcopy(
        x_ref.at[1, hand_slot, theirs], x_ref.at[1, last - get_slot, theirs],
        s_f.at[0], r_f.at[0], cpeer,
    )

    acc[...] = jnp.zeros_like(acc)
    lacc[...] = jnp.zeros_like(lacc)
    in_k.wait()
    in_t.wait()
    for k in range(mdev + 1):
        own_copy(k).wait()

    @pl.when(outer)
    def _():
        own_copy(mdev + 1).wait()

    for d in (0, 1, 2, 3):
        for side in range(2):
            edge_of(side, d, ens_at(d)).wait_recv()
    lef[...] = lei[...].astype(F32)

    col = lax.broadcasted_iota(jnp.int32, (cols, chans), 0)

    def shift(ref, slot, edge):
        for mem in range(members):
            v = ref[1, slot, mem].astype(F32)
            lo = jnp.where(col == 0, edge(0, mem), pltpu.roll(v, 1, 0))
            hi = jnp.where(col == cols - 1, edge(1, mem), pltpu.roll(v, cols - 1, 0))
            ref[0, slot, mem] = lo.astype(BF16)
            ref[2, slot, mem] = hi.astype(BF16)

    def ready(q):
        for d in range(1, 4):
            src = ens_at(d)
            there = (src // 2) != xx
            exists = ((q < last) | outer) & ((q > 0) | jnp.logical_not(there))

            @pl.when(exists)
            def _():
                row_of(d, e, q, src).wait_recv()

        @pl.when(q == 0)
        def _():
            hand.wait_recv()

        @pl.when(q == 1)
        def _():
            hand.start()

        slot = slot_of(core, q)
        shift(
            x_ref, slot,
            lambda side, mem: lef[side, mem // mdev, pl.ds(slot * mdev + mem % mdev, 1)],
        )

    def smooth(gap):
        square = gap * gap + smoothing * smoothing
        inv = lax.rsqrt(square)
        return gap * inv, square * inv

    def fields_of(i):
        total = None
        for a in range(3):
            for b in range(3):
                w = x_ref[b, i + a].reshape(cells, chans)
                term = jnp.dot(w, kv[a * 3 + b], preferred_element_type=F32)
                total = term if total is None else total + term
        fld[...] = total.reshape(members, cols, chans)

    def pairs_of(i):
        for blk in range(cols // 16):
            for lane in range(chans // 128):
                ln = pl.ds(lane * 128, 128)
                at = pl.ds(blk * 16, 16)
                tgt = tv[i, at, ln].astype(F32)
                f = [fld[m, at, ln] for m in range(members)]
                sums = [None] * members
                pair_w = None
                for m in range(members):
                    for o in range(m + 1, members):
                        sl, w = smooth(f[m] - f[o])
                        sums[m] = sl if sums[m] is None else sums[m] + sl
                        sums[o] = -sl if sums[o] is None else sums[o] - sl
                        pair_w = w if pair_w is None else pair_w + w
                own_w = None
                for m in range(members):
                    own_s, w = smooth(f[m] - tgt)
                    own_w = w if own_w is None else own_w + w
                    sl = own_s * (1.0 / members) - sums[m] * (1.0 / (members * (members - 1)))
                    sp[1, 1 + i, m, at, ln] = sl.astype(BF16)
                    if blk == 0:
                        eo[0, i, m : m + 1, ln] = sl[0:1]
                    if blk == cols // 16 - 1:
                        eo[1, i, m : m + 1, ln] = sl[15:16]
                lacc[:, ln] += own_w * (1.0 / members) - pair_w * (
                    1.0 / (members * (members - 1))
                )

    def kernel_terms(pair):
        i = base_of(pair)
        slt = sp[1, pl.ds(1 + i, 2)].reshape(2 * cells, chans).astype(F32).T.astype(BF16)
        for tap in range(TAPS):
            a, b = tap // 3, tap % 3
            w = x_ref[b, pl.ds(i + a, 2)].reshape(2 * cells, chans)
            p = jnp.dot(slt, w, preferred_element_type=F32)
            for h in range(2):
                acc[h, tap] += p[:, h * 128 : h * 128 + 128]

    inner_halo = rcopy(
        sp.at[1, hand_slot], sp.at[1, last - get_slot], s_h.at[0], r_h.at[0], cpeer
    )
    outer_slot = slot_of(core, own)
    outer_halo = rcopy(
        sp.at[1, outer_slot], sp.at[1, last - slot_of(core, last)], s_h.at[1], r_h.at[1], across
    )
    edges = [
        rcopy(eo.at[1], ei.at[0], s_e.at[0], r_e.at[0], {"space": right_s}),
        rcopy(eo.at[0], ei.at[1], s_e.at[1], r_e.at[1], {"space": left_s}),
    ]

    @pl.loop(0, len(BLOCKS))
    def _(blk):
        start = jnp.int32(BLOCKS[0][0])
        stop = jnp.int32(BLOCKS[0][1])
        for k in range(1, len(BLOCKS)):
            start = jnp.where(blk == k, BLOCKS[k][0], start)
            stop = jnp.where(blk == k, BLOCKS[k][1], stop)
        first = jnp.where(blk == 0, 0, start + 2)

        @pl.loop(first, stop + 2)
        def _(t):
            ready(jnp.where(t < 3, lax.rem(t + 1, 3), t))

            @pl.when(t >= 2)
            def _():
                i = slot_of(core, t - 1) - 1
                fields_of(i)
                pairs_of(i)

            @pl.when(t == 2)
            def _():
                inner_halo.start()

            @pl.when(t == last)
            def _():
                for c in edges:
                    c.start()

                @pl.when(outer)
                def _():
                    outer_halo.start()

        @pl.loop(start // 2, stop // 2)
        def _(pair):
            kernel_terms(pair)

    def rows_at(p, h, first=0, count=None):
        start = p * span + h * half + first
        return pl.ds(pl.multiple_of(start, 16), half if count is None else count)

    taps_of = []
    done = 0
    for p in range(pieces):
        upto = min(TAPS, -(-(p + 1) * span // 128))
        taps_of.append((done, upto))
        done = upto

    by_core = []
    for p, (t0, t1) in enumerate(taps_of):
        if t1 > t0:
            by_core.append(
                rcopy(
                    acc.at[1 - core, pl.ds(t0, t1 - t0)], r1.at[pl.ds(t0, t1 - t0)],
                    s_c.at[p], r_c.at[p], cpeer,
                )
            )
            by_core[-1].start()
        else:
            by_core.append(None)

    total = lacc[...]
    total = total[0:8, 0:128] + total[8:16, 0:128] + total[0:8, 128:256] + total[8:16, 128:256]
    l1[...] = total
    ls_core = rcopy(l1, lr1, s_ls.at[0], r_ls.at[0], cpeer)
    ls_core.start()
    if pieces * span > TAPS * 128:
        tail = pl.ds(TAPS * 128, pieces * span - TAPS * 128)
        g[tail] = jnp.zeros((pieces * span - TAPS * 128, chans), F32)
        b2[tail] = jnp.zeros((pieces * span - TAPS * 128, chans), BF16)

    def by_y(p):
        there = rows_at(p, 1 - sy)
        return rcopy(b2.at[there], r2.at[there], s_y.at[p], r_y.at[p], ypeer)

    def y_here(p):
        here = rows_at(p, sy)
        return rcopy(b2.at[here], r2.at[here], s_y.at[p], r_y.at[p], ypeer)

    for p, (t0, t1) in enumerate(taps_of):
        if by_core[p] is not None:
            by_core[p].wait_recv()

            @pl.loop(t0, t1)
            def _(tap):
                v = (acc[core, tap] + r1[tap]).T
                at = pl.ds(pl.multiple_of(tap * 128, 128), 128)
                g[at] = v
                b2[at] = v.astype(BF16)

        by_y(p).start()

    ls_core.wait_recv()
    l2[...] = l1[...] + lr1[...]
    ls_x = rcopy(l2, lr2, s_ls.at[1], r_ls.at[1], xpeer)
    ls_x.start()

    for c in edges:
        c.wait_recv()
    hand_edge = rcopy(ei.at[:, hand_slot - 1], eh.at[0], s_h.at[2], r_h.at[2], cpeer)
    outer_edge = rcopy(ei.at[:, outer_slot - 1], eh.at[1], s_h.at[3], r_h.at[3], across)
    hand_edge.start()

    @pl.when(outer)
    def _():
        outer_edge.start()

    @pl.loop(0, own)
    def _(i):
        shift(sp, 1 + i, lambda side, mem: ei[side, i, mem : mem + 1])

    inner_halo.wait_recv()
    hand_edge.wait_recv()

    def by_z(p, d, src):
        to = lax.rem(sz + d, nz)
        return rcopy(
            b3.at[pl.ds(pl.multiple_of((p * nz + to) * part, 16), part)],
            r3.at[src, pl.ds(pl.multiple_of(p * part, 16), part)],
            s_z.at[p, d], r_z.at[p, src], {"space": to * 2 + sy},
        )

    def give(d, pair, to, src):
        i = base_of(pair)
        return rcopy(
            gib.at[pl.ds(to * mdev, mdev), pl.ds(i, 2)],
            gi_ref.at[:, pl.ds(src * own + i, 2)],
            s_g.at[d, pair], r_g.at[src, pair], {"ens": to},
        )

    def taken(d, pair):
        src = ens_at(d)
        i = jnp.where(lax.rem(src, 2) == 0, own - 2 - 2 * pair, 2 * pair)
        return rcopy(
            gib.at[pl.ds(e * mdev, mdev), pl.ds(i, 2)],
            gi_ref.at[:, pl.ds(src * own + i, 2)],
            s_g.at[d, pair], r_g.at[src, pair], {"ens": e},
        )

    @pl.loop(0, own // 2)
    def _(pair):
        @pl.when((pair == 0) | ((pair == own // 2 - 1) & outer))
        def _():
            @pl.when(pair > 0)
            def _():
                outer_halo.wait_recv()
                outer_edge.wait_recv()

            k = jnp.where(pair == 0, 0, 1)
            shift(
                sp, slot_of(core, jnp.where(pair == 0, 0, last)),
                lambda side, mem: eh[k, side, mem : mem + 1],
            )

        i = base_of(pair)
        total = None
        for a in range(3):
            for b in range(3):
                w = sp[2 - b, pl.ds(i + 2 - a, 2)].reshape(2 * cells, chans)
                term = lax.dot_general(w, kv[a * 3 + b], NT, preferred_element_type=F32)
                total = term if total is None else total + term
        total = total.reshape(2, members, cols, chans).astype(BF16)
        for r in range(2):
            gib[:, i + r] = total[r]
        for d in (2, 3, 1):
            give(d, pair, ens_at(d), e).start()
        for m in range(mdev):
            gi_ref[m, pl.ds(e * own + i, 2)] = gib[e * mdev + m, pl.ds(i, 2)]

        p = pair - 1

        @pl.when((p >= 0) & (p < pieces))
        def _():
            y_here(p).wait_recv()
            here = rows_at(p, sy)
            total = g[here] + r2[here].astype(F32)
            g[here] = total
            b3[pl.ds(pl.multiple_of(p * half, 16), half)] = total.astype(BF16)

            @pl.loop(1, nz)
            def _(d):
                by_z(p, d, sz).start()

    ls_x.wait_recv()
    l3[...] = l2[...] + lr2[...]

    def loss_to_strip(d, i):
        return rcopy(l3, lr3.at[i], s_lp.at[d], r_lp.at[i], {"space": lax.rem(s + d, n)})

    @pl.loop(1, n)
    def _(d):
        loss_to_strip(d, s).start()

    def by_x(p):
        at = pl.ds(p * part, part)
        return rcopy(b4.at[at], r4.at[at], s_v.at[p], r_v.at[p], xpeer)

    def back_z(p, d, src):
        mine = gk_ref.at[core, rows_at(p, sy, src * part, part)]
        to = lax.rem(sz + d, nz)
        return rcopy(mine, mine, s_az.at[p, d], r_az.at[p, src], {"space": to * 2 + sy})

    def back_y(p, h):
        mine = gk_ref.at[core, rows_at(p, h)]
        return rcopy(mine, mine, s_ay.at[p], r_ay.at[p], ypeer)

    def back_core(p, c, h, k):
        mine = gk_ref.at[c, rows_at(p, h)]
        return rcopy(mine, mine, s_ac.at[p, k], r_ac.at[p, k], cpeer)

    def step_z(p):
        def take(d, v):
            src = lax.rem(sz + d, nz)
            by_z(p, d, src).wait_recv()
            return v + r3[src, pl.ds(p * part, part)].astype(F32)

        v = lax.fori_loop(1, nz, take, g[rows_at(p, sy, sz * part, part)])
        b4[pl.ds(p * part, part)] = v.astype(BF16)
        by_x(p).start()

    def step_x(p):
        by_x(p).wait_recv()
        at = pl.ds(p * part, part)
        v = b4[at].astype(F32) + r4[at].astype(F32)
        gk_ref[core, rows_at(p, sy, sz * part, part)] = v.astype(BF16)

        @pl.loop(1, nz)
        def _(d):
            back_z(p, d, sz).start()

    def step_back_z(p):
        @pl.loop(1, nz)
        def _(d):
            back_z(p, d, lax.rem(sz + d, nz)).wait_recv()

        back_y(p, sy).start()
        back_core(p, core, sy, 0).start()

    def step_back_y(p):
        back_y(p, 1 - sy).wait_recv()
        back_core(p, core, 1 - sy, 1).start()

    stages = (step_z, step_x, step_back_z, step_back_y)
    order = [(2 * k + p + (k > 1), k, p) for k in range(4) for p in range(pieces)]
    for _, k, p in sorted(order):
        stages[k](p)

    def take_loss(d, v):
        i = lax.rem(s + d, n)
        loss_to_strip(d, i).wait_recv()
        return v + lr3[i]

    loss_ref[...] = lax.fori_loop(1, n, take_loss, l3[...])

    @pl.loop(0, own // 2)
    def _(pair):
        for d in range(1, 4):
            give(d, pair, ens_at(d), e).wait_send()
            taken(d, pair).wait_recv()

    for p in range(pieces):
        back_core(p, 1 - core, sy, 0).wait_recv()
        back_core(p, 1 - core, 1 - sy, 1).wait_recv()

    @pl.loop(0, last + 1)
    def _(q):
        for d in range(1, 4):
            to = ens_at(d)

            @pl.when(goes(to, q))
            def _():
                row_of(d, to, q, e).wait_send()

    for d in range(4):
        for side in range(2):
            edge_of(side, d, e).wait_send()

    @pl.when(outer)
    def _():
        outer_halo.wait_send()
        outer_edge.wait_send()

    @pl.loop(1, n)
    def _(d):
        loss_to_strip(d, s).wait_send()

    @pl.loop(1, nz)
    def _(d):
        for p in range(pieces):
            by_z(p, d, sz).wait_send()
            back_z(p, d, sz).wait_send()

    for p in range(pieces):
        if by_core[p] is not None:
            by_core[p].wait_send()
        by_y(p).wait_send()
        by_x(p).wait_send()
        back_y(p, sy).wait_send()
        back_core(p, core, sy, 0).wait_send()
        back_core(p, core, 1 - sy, 1).wait_send()
    for c in edges + [hand, inner_halo, hand_edge, ls_core, ls_x]:
        c.wait_send()


def finish(scale, loss_scale, gi_ref, gk_ref, l_ref, gi_out, gk_out, loss_out, wide, sem):
    taps = wide.shape[0]
    out_gi = pltpu.make_async_copy(gi_ref, gi_out, sem.at[taps])
    out_gi.start()

    def out_tap(tap):
        return pltpu.make_async_copy(wide.at[tap], gk_out.at[tap], sem.at[tap])

    for tap in range(taps):
        for h in range(2):
            v = gk_ref[h, tap * 128 : tap * 128 + 128].astype(F32)
            wide[tap, h * 128 : h * 128 + 128] = v * scale
        out_tap(tap).start()
    loss_out[0, 0] = jnp.sum(l_ref[...]) * loss_scale
    for tap in range(taps):
        out_tap(tap).wait()
    out_gi.wait()


def local(n, latents, targets, kernel):
    mdev, rows, cols, chans = latents.shape
    members = mdev * 4
    own = rows // 4
    slots = own + 2
    pieces, part = pieces_of(n)
    nz = n // 2
    hp = pieces * part * n
    vmem, dma = pltpu.VMEM, pltpu.SemaphoreType.DMA
    hbm = pl.BlockSpec(memory_space=pltpu.HBM)
    on_chip = pl.BlockSpec(memory_space=vmem)
    shifted = vmem((3, slots, members, cols, chans), BF16)
    edge = vmem((2, own, members, chans), F32)
    tile = vmem((8, 128), F32)
    edge_rows = -(-((rows - own) * mdev + 32) // 16) * 16
    gi, gk, loss = pl.pallas_call(
        functools.partial(body, n, members),
        name="crps_step",
        out_shape=(
            jax.ShapeDtypeStruct(latents.shape, BF16),
            jax.ShapeDtypeStruct((2, hp, chans), BF16),
            jax.ShapeDtypeStruct((8, 128), F32),
        ),
        in_specs=[hbm] * 3,
        out_specs=(on_chip,) * 3,
        scratch_shapes=[
            shifted,
            vmem((mdev, rows, cols, chans), BF16),
            vmem((own, cols, chans), BF16),
            vmem((TAPS, chans, chans), BF16),
            vmem((2, edge_rows, chans), F32),
            vmem((2, edge_rows, chans), BF16),
            vmem((2, 4, 32, chans), BF16),
            vmem((2, 4, 32, chans), F32),
            vmem((members, cols, chans), F32),
            shifted,
            vmem((2, TAPS, chans, 128), F32),
            edge, edge,
            vmem((2, 2, members, chans), F32),
            vmem((members, own, cols, chans), BF16),
            vmem((16, chans), F32),
            vmem((TAPS, chans, 128), F32),
            vmem((hp, chans), F32),
            vmem((hp, chans), BF16),
            vmem((hp, chans), BF16),
            vmem((hp // 2, chans), BF16),
            vmem((nz, pieces * part, chans), BF16),
            vmem((pieces * part, chans), BF16),
            vmem((pieces * part, chans), BF16),
            tile, tile, tile, tile, tile,
            vmem((n, 8, 128), F32),
            dma((3,)), dma((mdev + 2,)),
            dma((4, slots)), dma((4, slots)), dma((1,)), dma((1,)),
            dma((2, 4)), dma((2, 4)), dma((2,)), dma((2,)), dma((4,)), dma((4,)),
            dma((4, own // 2)), dma((4, own // 2)),
            dma((pieces,)), dma((pieces,)), dma((pieces,)), dma((pieces,)),
            dma((pieces, nz)), dma((pieces, nz)), dma((pieces,)), dma((pieces,)),
            dma((pieces, nz)), dma((pieces, nz)), dma((pieces,)), dma((pieces,)),
            dma((pieces, 2)), dma((pieces, 2)),
            dma((2,)), dma((2,)), dma((n,)), dma((n,)),
        ],
        compiler_params=pltpu.CompilerParams(
            collective_id=0, has_side_effects=True, vmem_limit_bytes=48 * 2**20
        ),
    )(latents, targets, kernel.reshape(TAPS, chans, chans))
    longitude = cols * n
    gi, gk, loss = pl.pallas_call(
        functools.partial(
            finish, 1.0 / (members * rows * longitude), 1.0 / (rows * longitude * chans)
        ),
        name="finish",
        out_shape=(
            jax.ShapeDtypeStruct(latents.shape, BF16),
            jax.ShapeDtypeStruct((TAPS, chans, chans), F32),
            jax.ShapeDtypeStruct((1, 1), F32),
        ),
        in_specs=[on_chip] * 3,
        out_specs=(hbm, hbm, pl.BlockSpec(memory_space=pltpu.SMEM)),
        scratch_shapes=[vmem((TAPS, chans, chans), F32), dma((TAPS + 1,))],
        compiler_params=pltpu.CompilerParams(vmem_limit_bytes=24 * 2**20),
    )(gi, gk, loss)
    return loss.reshape(()), gi, gk.reshape(3, 3, chans, chans)


def solution(mesh):
    in_specs = (P("ens", None, "space", None), P(None, "space", None), P())
    out_specs = (P(), P("ens", None, "space", None), P())
    return jax.shard_map(
        functools.partial(local, mesh.shape["space"]),
        mesh=mesh, in_specs=in_specs, out_specs=out_specs, check_vma=False,
    )
```

```python
import functools

import jax
import jax.numpy as jnp
from jax import lax
from jax.experimental import pallas as pl
from jax.experimental.pallas import tpu as pltpu
from jax.sharding import PartitionSpec as P

smoothing = 0.1
F32, BF16 = jnp.float32, jnp.bfloat16
NT = (((1,), (1,)), ((), ()))
TAPS = 9
BLOCKS = ((0, 4), (4, 8))


def pieces_of(n):
    units = -(-TAPS * 128 // (16 * n))
    pieces = min(TAPS, units)
    return pieces, 16 * -(-units // pieces)


def body(
    n, members,
    lat_hbm, t_hbm, k_hbm,
    gi_ref, gk_ref, loss_ref,
    x_ref, latv, tv, kv, lef32, leo, lei, lef, fld, sp, acc, eo, ei, eh, gib, lacc,
    r1, g, b2, r2, b3, r3, b4, r4, l1, lr1, l2, lr2, l3, lr3,
    s_in, s_own, s_x, r_x, s_f, r_f, s_le, r_le, s_e, r_e, s_h, r_h, s_g, r_g,
    s_c, r_c, s_y, r_y, s_z, r_z, s_v, r_v, s_az, r_az, s_ay, r_ay, s_ac, r_ac,
    s_ls, r_ls, s_lp, r_lp,
):
    mdev, rows, cols, chans = lat_hbm.shape
    own = rows // 4
    last = own + 1
    cells = members * cols
    pieces, part = pieces_of(n)
    nz = n // 2
    half = part * nz
    span = 2 * half
    e = lax.axis_index("ens")
    s = lax.axis_index("space")
    core = lax.rem(e, 2)
    xx = e // 2
    sy = lax.rem(s, 2)
    sz = s // 2
    outer = xx != core
    cpeer = {"ens": xx * 2 + (1 - core)}
    xpeer = {"ens": (1 - xx) * 2 + core}
    across = {"ens": 3 - e}
    ypeer = {"space": sz * 2 + (1 - sy)}
    right_s = lax.rem(s + 1, n)
    left_s = lax.rem(s + n - 1, n)
    MESH = pl.DeviceIdType.MESH

    def rcopy(src, dst, ss, rs, dev):
        return pltpu.make_async_remote_copy(
            src_ref=src, dst_ref=dst, send_sem=ss, recv_sem=rs,
            device_id=dev, device_id_type=MESH,
        )

    def ens_at(d):
        return lax.rem(e + d, 4)

    def slot_of(c, q):
        return jnp.where(c == 0, last - q, q)

    def base_of(pair):
        return jnp.where(core == 0, own - 2 - 2 * pair, 2 * pair)

    in_lat = pltpu.make_async_copy(lat_hbm, latv, s_in.at[0])
    in_k = pltpu.make_async_copy(k_hbm, kv, s_in.at[1])
    in_t = pltpu.make_async_copy(t_hbm.at[pl.ds(e * own, own)], tv, s_in.at[2])
    in_lat.start()
    in_k.start()
    in_t.start()
    barrier = pltpu.get_barrier_semaphore()
    for d in range(1, 4):
        for strip in (s, right_s, left_s):
            pl.semaphore_signal(
                barrier, inc=1, device_id={"ens": ens_at(d), "space": strip}, device_id_type=MESH
            )

    @pl.loop(1, n)
    def _(d):
        pl.semaphore_signal(
            barrier, inc=1, device_id={"space": lax.rem(s + d, n)}, device_id_type=MESH
        )

    def own_copy(k):
        if k < mdev:
            return pltpu.make_async_copy(
                lat_hbm.at[k, pl.ds(e * own, own)], x_ref.at[1, pl.ds(1, own), e * mdev + k],
                s_own.at[k],
            )
        slot = slot_of(core, 0 if k == mdev else last)
        row = jnp.clip(e * own - 1 + slot, 0, rows - 1)
        return pltpu.make_async_copy(
            lat_hbm.at[:, row], x_ref.at[1, slot, pl.ds(e * mdev, mdev)], s_own.at[k]
        )

    for k in range(mdev + 1):
        own_copy(k).start()

    @pl.when(outer)
    def _():
        own_copy(mdev + 1).start()

    pl.semaphore_wait(barrier, n - 1 + 9)

    def row_of(d, to, q, src):
        slot = slot_of(lax.rem(to, 2), q)
        row = jnp.clip(to * own - 1 + slot, 0, rows - 1)
        return rcopy(
            lat_hbm.at[:, row], x_ref.at[1, slot, pl.ds(mdev * src, mdev)],
            s_x.at[d, q], r_x.at[src, q], {"ens": to},
        )

    def goes(to, q):
        there = (to // 2) != xx
        exists = (q < last) | ((to // 2) != lax.rem(to, 2))
        return exists & ((q > 0) | jnp.logical_not(there))

    def edge_of(side, d, src):
        to = ens_at(d)
        return rcopy(
            leo.at[side, pl.ds(pl.multiple_of(to * own * mdev, 16), 32)], lei.at[1 - side, src],
            s_le.at[side, d], r_le.at[1 - side, src],
            {"ens": to, "space": left_s if side == 0 else right_s},
        )

    def send_rows(first, stop):
        @pl.loop(first, stop)
        def _(j):
            q = jnp.where(j < 3, lax.rem(j + 1, 3), j)
            for d in (2, 3, 1):
                to = ens_at(d)

                @pl.when(goes(to, q))
                def _():
                    row_of(d, to, q, e).start()

    send_rows(0, 3)
    lef32[...] = jnp.zeros_like(lef32)
    in_lat.wait()

    @pl.loop(0, rows)
    def _(row):
        for m in range(mdev):
            v = latv[m, row, 0:16].astype(F32)
            w = latv[m, row, cols - 16 : cols].astype(F32)
            lef32[0, pl.ds((1 + row) * mdev + m, 1)] = v[0:1]
            lef32[1, pl.ds((1 + row) * mdev + m, 1)] = w[15:16]

    leo[...] = lef32[...].astype(BF16)
    for d in (2, 3, 1, 0):
        for side in range(2):
            edge_of(side, d, e).start()
    send_rows(3, last + 1)

    @pl.when(jnp.logical_not(outer))
    def _():
        blank = jnp.zeros((members, cols, chans), BF16)
        slot = slot_of(core, last)
        x_ref[1, slot] = blank
        for c in range(3):
            sp[c, slot] = blank

    hand_slot = slot_of(core, 1)
    get_slot = slot_of(core, 0)
    theirs = pl.ds(2 * mdev * (1 - xx), 2 * mdev)
    hand = rcopy(
        x_ref.at[1, hand_slot, theirs], x_ref.at[1, last - get_slot, theirs],
        s_f.at[0], r_f.at[0], cpeer,
    )

    acc[...] = jnp.zeros_like(acc)
    lacc[...] = jnp.zeros_like(lacc)
    in_k.wait()
    in_t.wait()
    for k in range(mdev + 1):
        own_copy(k).wait()

    @pl.when(outer)
    def _():
        own_copy(mdev + 1).wait()

    for d in (0, 1, 2, 3):
        for side in range(2):
            edge_of(side, d, ens_at(d)).wait_recv()
    lef[...] = lei[...].astype(F32)

    col = lax.broadcasted_iota(jnp.int32, (cols, chans), 0)

    def shift(ref, slot, edge):
        for mem in range(members):
            v = ref[1, slot, mem].astype(F32)
            lo = jnp.where(col == 0, edge(0, mem), pltpu.roll(v, 1, 0))
            hi = jnp.where(col == cols - 1, edge(1, mem), pltpu.roll(v, cols - 1, 0))
            ref[0, slot, mem] = lo.astype(BF16)
            ref[2, slot, mem] = hi.astype(BF16)

    def ready(q):
        for d in range(1, 4):
            src = ens_at(d)
            there = (src // 2) != xx
            exists = ((q < last) | outer) & ((q > 0) | jnp.logical_not(there))

            @pl.when(exists)
            def _():
                row_of(d, e, q, src).wait_recv()

        @pl.when(q == 0)
        def _():
            hand.wait_recv()

        @pl.when(q == 1)
        def _():
            hand.start()

        slot = slot_of(core, q)
        shift(
            x_ref, slot,
            lambda side, mem: lef[side, mem // mdev, pl.ds(slot * mdev + mem % mdev, 1)],
        )

    def smooth(gap):
        square = gap * gap + smoothing * smoothing
        inv = lax.rsqrt(square)
        return gap * inv, square * inv

    def fields_of(i):
        total = None
        for a in range(3):
            for b in range(3):
                w = x_ref[b, i + a].reshape(cells, chans)
                term = jnp.dot(w, kv[a * 3 + b], preferred_element_type=F32)
                total = term if total is None else total + term
        fld[...] = total.reshape(members, cols, chans)

    def pairs_of(i):
        for blk in range(cols // 16):
            for lane in range(chans // 128):
                ln = pl.ds(lane * 128, 128)
                at = pl.ds(blk * 16, 16)
                tgt = tv[i, at, ln].astype(F32)
                f = [fld[m, at, ln] for m in range(members)]
                sums = [None] * members
                pair_w = None
                for m in range(members):
                    for o in range(m + 1, members):
                        sl, w = smooth(f[m] - f[o])
                        sums[m] = sl if sums[m] is None else sums[m] + sl
                        sums[o] = -sl if sums[o] is None else sums[o] - sl
                        pair_w = w if pair_w is None else pair_w + w
                own_w = None
                for m in range(members):
                    own_s, w = smooth(f[m] - tgt)
                    own_w = w if own_w is None else own_w + w
                    sl = own_s * (1.0 / members) - sums[m] * (1.0 / (members * (members - 1)))
                    sp[1, 1 + i, m, at, ln] = sl.astype(BF16)
                    if blk == 0:
                        eo[0, i, m : m + 1, ln] = sl[0:1]
                    if blk == cols // 16 - 1:
                        eo[1, i, m : m + 1, ln] = sl[15:16]
                lacc[:, ln] += own_w * (1.0 / members) - pair_w * (
                    1.0 / (members * (members - 1))
                )

    def kernel_terms(pair):
        i = base_of(pair)
        slt = sp[1, pl.ds(1 + i, 2)].reshape(2 * cells, chans).astype(F32).T.astype(BF16)
        for tap in range(TAPS):
            a, b = tap // 3, tap % 3
            w = x_ref[b, pl.ds(i + a, 2)].reshape(2 * cells, chans)
            p = jnp.dot(slt, w, preferred_element_type=F32)
            for h in range(2):
                acc[h, tap] += p[:, h * 128 : h * 128 + 128]

    inner_halo = rcopy(
        sp.at[1, hand_slot], sp.at[1, last - get_slot], s_h.at[0], r_h.at[0], cpeer
    )
    outer_slot = slot_of(core, own)
    outer_halo = rcopy(
        sp.at[1, outer_slot], sp.at[1, last - slot_of(core, last)], s_h.at[1], r_h.at[1], across
    )
    edges = [
        rcopy(eo.at[1], ei.at[0], s_e.at[0], r_e.at[0], {"space": right_s}),
        rcopy(eo.at[0], ei.at[1], s_e.at[1], r_e.at[1], {"space": left_s}),
    ]

    @pl.loop(0, len(BLOCKS))
    def _(blk):
        start = jnp.int32(BLOCKS[0][0])
        stop = jnp.int32(BLOCKS[0][1])
        for k in range(1, len(BLOCKS)):
            start = jnp.where(blk == k, BLOCKS[k][0], start)
            stop = jnp.where(blk == k, BLOCKS[k][1], stop)
        first = jnp.where(blk == 0, 0, start + 2)

        @pl.loop(first, stop + 2)
        def _(t):
            ready(jnp.where(t < 3, lax.rem(t + 1, 3), t))

            @pl.when(t >= 2)
            def _():
                i = slot_of(core, t - 1) - 1
                fields_of(i)
                pairs_of(i)

            @pl.when(t == 2)
            def _():
                inner_halo.start()

            @pl.when(t == last)
            def _():
                for c in edges:
                    c.start()

                @pl.when(outer)
                def _():
                    outer_halo.start()

        @pl.loop(start // 2, stop // 2)
        def _(pair):
            kernel_terms(pair)

    def rows_at(p, h, first=0, count=None):
        start = p * span + h * half + first
        return pl.ds(pl.multiple_of(start, 16), half if count is None else count)

    def first_tap(p):
        return jnp.minimum((p * span + 127) // 128, TAPS)

    def by_core(tap):
        return rcopy(acc.at[1 - core, tap], r1.at[tap], s_c.at[tap], r_c.at[tap], cpeer)

    for tap in range(TAPS):
        by_core(tap).start()

    total = lacc[...]
    total = total[0:8, 0:128] + total[8:16, 0:128] + total[0:8, 128:256] + total[8:16, 128:256]
    l1[...] = total
    ls_core = rcopy(l1, lr1, s_ls.at[0], r_ls.at[0], cpeer)
    ls_core.start()
    if pieces * span > TAPS * 128:
        tail = pl.ds(TAPS * 128, pieces * span - TAPS * 128)
        g[tail] = jnp.zeros((pieces * span - TAPS * 128, chans), F32)
        b2[tail] = jnp.zeros((pieces * span - TAPS * 128, chans), BF16)

    def by_y(p):
        there = rows_at(p, 1 - sy)
        return rcopy(b2.at[there], r2.at[there], s_y.at[p], r_y.at[p], ypeer)

    def y_here(p):
        here = rows_at(p, sy)
        return rcopy(b2.at[here], r2.at[here], s_y.at[p], r_y.at[p], ypeer)

    @pl.loop(0, pieces)
    def _(p):
        @pl.loop(first_tap(p), first_tap(p + 1))
        def _(tap):
            by_core(tap).wait_recv()
            v = (acc[core, tap] + r1[tap]).T
            at = pl.ds(pl.multiple_of(tap * 128, 128), 128)
            g[at] = v
            b2[at] = v.astype(BF16)

        by_y(p).start()

    ls_core.wait_recv()
    l2[...] = l1[...] + lr1[...]
    ls_x = rcopy(l2, lr2, s_ls.at[1], r_ls.at[1], xpeer)
    ls_x.start()

    for c in edges:
        c.wait_recv()
    hand_edge = rcopy(ei.at[:, hand_slot - 1], eh.at[0], s_h.at[2], r_h.at[2], cpeer)
    outer_edge = rcopy(ei.at[:, outer_slot - 1], eh.at[1], s_h.at[3], r_h.at[3], across)
    hand_edge.start()

    @pl.when(outer)
    def _():
        outer_edge.start()

    @pl.loop(0, own)
    def _(i):
        shift(sp, 1 + i, lambda side, mem: ei[side, i, mem : mem + 1])

    inner_halo.wait_recv()
    hand_edge.wait_recv()

    def by_z(p, d, src):
        to = lax.rem(sz + d, nz)
        return rcopy(
            b3.at[pl.ds(pl.multiple_of((p * nz + to) * part, 16), part)],
            r3.at[src, pl.ds(pl.multiple_of(p * part, 16), part)],
            s_z.at[p, d], r_z.at[p, src], {"space": to * 2 + sy},
        )

    def give(d, pair, to, src):
        i = base_of(pair)
        return rcopy(
            gib.at[pl.ds(to * mdev, mdev), pl.ds(i, 2)],
            gi_ref.at[:, pl.ds(src * own + i, 2)],
            s_g.at[d, pair], r_g.at[src, pair], {"ens": to},
        )

    def taken(d, pair):
        src = ens_at(d)
        i = jnp.where(lax.rem(src, 2) == 0, own - 2 - 2 * pair, 2 * pair)
        return rcopy(
            gib.at[pl.ds(e * mdev, mdev), pl.ds(i, 2)],
            gi_ref.at[:, pl.ds(src * own + i, 2)],
            s_g.at[d, pair], r_g.at[src, pair], {"ens": e},
        )

    def grad_in(pair):
        @pl.when((pair == 0) | ((pair == own // 2 - 1) & outer))
        def _():
            @pl.when(pair > 0)
            def _():
                outer_halo.wait_recv()
                outer_edge.wait_recv()

            k = jnp.where(pair == 0, 0, 1)
            shift(
                sp, slot_of(core, jnp.where(pair == 0, 0, last)),
                lambda side, mem: eh[k, side, mem : mem + 1],
            )

        i = base_of(pair)
        total = None
        for a in range(3):
            for b in range(3):
                w = sp[2 - b, pl.ds(i + 2 - a, 2)].reshape(2 * cells, chans)
                term = lax.dot_general(w, kv[a * 3 + b], NT, preferred_element_type=F32)
                total = term if total is None else total + term
        total = total.reshape(2, members, cols, chans).astype(BF16)
        for r in range(2):
            gib[:, i + r] = total[r]
        for m in range(mdev):
            gi_ref[m, pl.ds(e * own + i, 2)] = gib[e * mdev + m, pl.ds(i, 2)]

    def give_all(pair):
        for d in (2, 3, 1):
            give(d, pair, ens_at(d), e).start()

    def loss_to_strip(d, i):
        return rcopy(l3, lr3.at[i], s_lp.at[d], r_lp.at[i], {"space": lax.rem(s + d, n)})

    def by_x(p):
        at = pl.ds(pl.multiple_of(p * part, 16), part)
        return rcopy(b4.at[at], r4.at[at], s_v.at[p], r_v.at[p], xpeer)

    def back_z(p, d, src):
        mine = gk_ref.at[core, rows_at(p, sy, src * part, part)]
        to = lax.rem(sz + d, nz)
        return rcopy(mine, mine, s_az.at[p, d], r_az.at[p, src], {"space": to * 2 + sy})

    def back_y(p, h):
        mine = gk_ref.at[core, rows_at(p, h)]
        return rcopy(mine, mine, s_ay.at[p], r_ay.at[p], ypeer)

    def back_core(p, c, h, k):
        mine = gk_ref.at[c, rows_at(p, h)]
        return rcopy(mine, mine, s_ac.at[p, k], r_ac.at[p, k], cpeer)

    def step_y(p):
        y_here(p).wait_recv()
        here = rows_at(p, sy)
        total = g[here] + r2[here].astype(F32)
        g[here] = total
        b3[pl.ds(pl.multiple_of(p * half, 16), half)] = total.astype(BF16)

        @pl.loop(1, nz)
        def _(d):
            by_z(p, d, sz).start()

    def step_z(p):
        def take(d, v):
            src = lax.rem(sz + d, nz)
            by_z(p, d, src).wait_recv()
            return v + r3[src, pl.ds(pl.multiple_of(p * part, 16), part)].astype(F32)

        v = lax.fori_loop(1, nz, take, g[rows_at(p, sy, sz * part, part)])
        b4[pl.ds(pl.multiple_of(p * part, 16), part)] = v.astype(BF16)
        by_x(p).start()

    def step_x(p):
        by_x(p).wait_recv()
        at = pl.ds(pl.multiple_of(p * part, 16), part)
        v = b4[at].astype(F32) + r4[at].astype(F32)
        gk_ref[core, rows_at(p, sy, sz * part, part)] = v.astype(BF16)

        @pl.loop(1, nz)
        def _(d):
            back_z(p, d, sz).start()

    def step_back_z(p):
        @pl.loop(1, nz)
        def _(d):
            back_z(p, d, lax.rem(sz + d, nz)).wait_recv()

        back_y(p, sy).start()
        back_core(p, core, sy, 0).start()

    def step_back_y(p):
        back_y(p, 1 - sy).wait_recv()
        back_core(p, core, 1 - sy, 1).start()

    stages = ((step_y, 0), (step_z, 5), (step_x, 8), (step_back_z, 13), (step_back_y, 17))
    sent = 5 + pieces

    @pl.loop(0, 17 + pieces)
    def _(t):
        @pl.when((lax.rem(t, 2) == 0) & (t < own))
        def _():
            pair = t // 2
            grad_in(pair)

            @pl.when(pair < 2)
            def _():
                give_all(pair)

        for stage, lag in stages:
            p = t - lag

            @pl.when((p >= 0) & (p < pieces))
            def _():
                stage(p)

        @pl.when(t == sent)
        def _():
            for pair in range(2, own // 2):
                give_all(pair)

            ls_x.wait_recv()
            l3[...] = l2[...] + lr2[...]

            @pl.loop(1, n)
            def _(d):
                loss_to_strip(d, s).start()

    def take_loss(d, v):
        i = lax.rem(s + d, n)
        loss_to_strip(d, i).wait_recv()
        return v + lr3[i]

    loss_ref[...] = lax.fori_loop(1, n, take_loss, l3[...])

    @pl.loop(0, own // 2)
    def _(pair):
        for d in range(1, 4):
            give(d, pair, ens_at(d), e).wait_send()
            taken(d, pair).wait_recv()

    @pl.loop(0, pieces)
    def _(p):
        back_core(p, 1 - core, sy, 0).wait_recv()
        back_core(p, 1 - core, 1 - sy, 1).wait_recv()

    @pl.loop(0, last + 1)
    def _(q):
        for d in range(1, 4):
            to = ens_at(d)

            @pl.when(goes(to, q))
            def _():
                row_of(d, to, q, e).wait_send()

    for d in range(4):
        for side in range(2):
            edge_of(side, d, e).wait_send()

    @pl.when(outer)
    def _():
        outer_halo.wait_send()
        outer_edge.wait_send()

    @pl.loop(1, n)
    def _(d):
        loss_to_strip(d, s).wait_send()

    @pl.loop(0, pieces)
    def _(p):
        by_y(p).wait_send()
        by_x(p).wait_send()
        back_y(p, sy).wait_send()
        back_core(p, core, sy, 0).wait_send()
        back_core(p, core, 1 - sy, 1).wait_send()

        @pl.loop(1, nz)
        def _(d):
            by_z(p, d, sz).wait_send()
            back_z(p, d, sz).wait_send()

    @pl.loop(0, TAPS)
    def _(tap):
        by_core(tap).wait_send()

    for c in edges + [hand, inner_halo, hand_edge, ls_core, ls_x]:
        c.wait_send()


def finish(scale, loss_scale, gi_ref, gk_ref, l_ref, gi_out, gk_out, loss_out, wide, sem):
    taps = wide.shape[0]
    out_gi = pltpu.make_async_copy(gi_ref, gi_out, sem.at[taps])
    out_gi.start()

    def out_tap(tap):
        return pltpu.make_async_copy(wide.at[tap], gk_out.at[tap], sem.at[tap])

    for tap in range(taps):
        for h in range(2):
            v = gk_ref[h, tap * 128 : tap * 128 + 128].astype(F32)
            wide[tap, h * 128 : h * 128 + 128] = v * scale
        out_tap(tap).start()
    loss_out[0, 0] = jnp.sum(l_ref[...]) * loss_scale
    for tap in range(taps):
        out_tap(tap).wait()
    out_gi.wait()


def local(n, latents, targets, kernel):
    mdev, rows, cols, chans = latents.shape
    members = mdev * 4
    own = rows // 4
    slots = own + 2
    pieces, part = pieces_of(n)
    nz = n // 2
    hp = pieces * part * n
    vmem, dma = pltpu.VMEM, pltpu.SemaphoreType.DMA
    hbm = pl.BlockSpec(memory_space=pltpu.HBM)
    on_chip = pl.BlockSpec(memory_space=vmem)
    shifted = vmem((3, slots, members, cols, chans), BF16)
    edge = vmem((2, own, members, chans), F32)
    tile = vmem((8, 128), F32)
    edge_rows = -(-((rows - own) * mdev + 32) // 16) * 16
    gi, gk, loss = pl.pallas_call(
        functools.partial(body, n, members),
        name="crps_step",
        out_shape=(
            vmem(latents.shape, BF16),
            vmem((2, hp, chans), BF16),
            vmem((8, 128), F32),
        ),
        in_specs=[hbm] * 3,
        out_specs=(on_chip,) * 3,
        scratch_shapes=[
            shifted,
            vmem((mdev, rows, cols, chans), BF16),
            vmem((own, cols, chans), BF16),
            vmem((TAPS, chans, chans), BF16),
            vmem((2, edge_rows, chans), F32),
            vmem((2, edge_rows, chans), BF16),
            vmem((2, 4, 32, chans), BF16),
            vmem((2, 4, 32, chans), F32),
            vmem((members, cols, chans), F32),
            shifted,
            vmem((2, TAPS, chans, 128), F32),
            edge, edge,
            vmem((2, 2, members, chans), F32),
            vmem((members, own, cols, chans), BF16),
            vmem((16, chans), F32),
            vmem((TAPS, chans, 128), F32),
            vmem((hp, chans), F32),
            vmem((hp, chans), BF16),
            vmem((hp, chans), BF16),
            vmem((hp // 2, chans), BF16),
            vmem((nz, pieces * part, chans), BF16),
            vmem((pieces * part, chans), BF16),
            vmem((pieces * part, chans), BF16),
            tile, tile, tile, tile, tile,
            vmem((n, 8, 128), F32),
            dma((3,)), dma((mdev + 2,)),
            dma((4, slots)), dma((4, slots)), dma((1,)), dma((1,)),
            dma((2, 4)), dma((2, 4)), dma((2,)), dma((2,)), dma((4,)), dma((4,)),
            dma((4, own // 2)), dma((4, own // 2)),
            dma((TAPS,)), dma((TAPS,)), dma((pieces,)), dma((pieces,)),
            dma((pieces, nz)), dma((pieces, nz)), dma((pieces,)), dma((pieces,)),
            dma((pieces, nz)), dma((pieces, nz)), dma((pieces,)), dma((pieces,)),
            dma((pieces, 2)), dma((pieces, 2)),
            dma((2,)), dma((2,)), dma((n,)), dma((n,)),
        ],
        compiler_params=pltpu.CompilerParams(
            collective_id=0, has_side_effects=True, vmem_limit_bytes=56 * 2**20
        ),
    )(latents, targets, kernel.reshape(TAPS, chans, chans))
    longitude = cols * n
    gi, gk, loss = pl.pallas_call(
        functools.partial(
            finish, 1.0 / (members * rows * longitude), 1.0 / (rows * longitude * chans)
        ),
        name="finish",
        out_shape=(
            jax.ShapeDtypeStruct(latents.shape, BF16),
            jax.ShapeDtypeStruct((TAPS, chans, chans), F32),
            jax.ShapeDtypeStruct((1, 1), F32),
        ),
        in_specs=[on_chip] * 3,
        out_specs=(hbm, hbm, pl.BlockSpec(memory_space=pltpu.SMEM)),
        scratch_shapes=[vmem((TAPS, chans, chans), F32), dma((TAPS + 1,))],
        compiler_params=pltpu.CompilerParams(vmem_limit_bytes=24 * 2**20),
    )(gi, gk, loss)
    return loss.reshape(()), gi, gk.reshape(3, 3, chans, chans)


def solution(mesh):
    in_specs = (P("ens", None, "space", None), P(None, "space", None), P())
    out_specs = (P(), P("ens", None, "space", None), P())
    return jax.shard_map(
        functools.partial(local, mesh.shape["space"]),
        mesh=mesh, in_specs=in_specs, out_specs=out_specs, check_vma=False,
    )
```

```python
import functools

import jax
import jax.numpy as jnp
from jax import lax
from jax.experimental import pallas as pl
from jax.experimental.pallas import tpu as pltpu
from jax.sharding import PartitionSpec as P

smoothing = 0.1
F32, BF16 = jnp.float32, jnp.bfloat16
NT = (((1,), (1,)), ((), ()))
TAPS = 9
EARLY, LATE_AT, LATE_STEP = 2, 12, 1
BLOCKS = ((0, 4), (4, 8))
ZFIRST = 2
ZLAG = (2, 8, 11, 15, 21)
GROUPS = ((0, 1, 2, 3, 4), (5, 6, 7, 8))


def pieces_of(n):
    units = -(-TAPS * 128 // (16 * n))
    pieces = min(TAPS, units)
    return pieces, 16 * -(-units // pieces)


def first_by_z(n):
    return ZFIRST if pieces_of(n)[0] == TAPS else 0


def body(
    n, members,
    lat_hbm, t_hbm, k_hbm,
    gi_ref, gk_ref, loss_ref,
    x_ref, latv, tv, kv, lef32, leo, lei, lef, fld, sp, acc, eo, eb, eib, ei, eh, gib, lacc, slt,
    r1, g, b2, r2, b3, r3, rz, b4, r4, l1, lr1, l2, lr2, l3, lr3,
    s_in, s_own, s_x, r_x, s_f, r_f, s_le, r_le, s_e, r_e, s_h, r_h, s_g, r_g,
    s_c, r_c, s_y, r_y, s_z, r_z, s_v, r_v, s_az, r_az, s_ay, r_ay, s_ac, r_ac,
    s_ls, r_ls, s_lp, r_lp,
):
    mdev, rows, cols, chans = lat_hbm.shape
    own = rows // 4
    last = own + 1
    cells = members * cols
    pieces, part = pieces_of(n)
    nz = n // 2
    zfirst = first_by_z(n)
    half = part * nz
    span = 2 * half
    e = lax.axis_index("ens")
    s = lax.axis_index("space")
    core = lax.rem(e, 2)
    xx = e // 2
    sy = lax.rem(s, 2)
    sz = s // 2
    outer = xx != core
    cpeer = {"ens": xx * 2 + (1 - core)}
    xpeer = {"ens": (1 - xx) * 2 + core}
    across = {"ens": 3 - e}
    ypeer = {"space": sz * 2 + (1 - sy)}
    right_s = lax.rem(s + 1, n)
    left_s = lax.rem(s + n - 1, n)
    MESH = pl.DeviceIdType.MESH

    def rcopy(src, dst, ss, rs, dev):
        return pltpu.make_async_remote_copy(
            src_ref=src, dst_ref=dst, send_sem=ss, recv_sem=rs,
            device_id=dev, device_id_type=MESH,
        )

    def ens_at(d):
        return lax.rem(e + d, 4)

    def slot_of(c, q):
        return jnp.where(c == 0, last - q, q)

    def base_of(pair):
        return jnp.where(core == 0, own - 2 - 2 * pair, 2 * pair)

    in_lat = pltpu.make_async_copy(lat_hbm, latv, s_in.at[0])
    in_k = pltpu.make_async_copy(k_hbm, kv, s_in.at[1])
    in_t = pltpu.make_async_copy(t_hbm.at[pl.ds(e * own, own)], tv, s_in.at[2])
    in_lat.start()
    in_k.start()
    in_t.start()
    barrier = pltpu.get_barrier_semaphore()
    for d in range(1, 4):
        for strip in (s, right_s, left_s):
            pl.semaphore_signal(
                barrier, inc=1, device_id={"ens": ens_at(d), "space": strip}, device_id_type=MESH
            )

    @pl.loop(1, n)
    def _(d):
        pl.semaphore_signal(
            barrier, inc=1, device_id={"space": lax.rem(s + d, n)}, device_id_type=MESH
        )

    def own_copy(k):
        if k < mdev:
            return pltpu.make_async_copy(
                lat_hbm.at[k, pl.ds(e * own, own)], x_ref.at[1, pl.ds(1, own), e * mdev + k],
                s_own.at[k],
            )
        slot = slot_of(core, 0 if k == mdev else last)
        row = jnp.clip(e * own - 1 + slot, 0, rows - 1)
        return pltpu.make_async_copy(
            lat_hbm.at[:, row], x_ref.at[1, slot, pl.ds(e * mdev, mdev)], s_own.at[k]
        )

    for k in range(mdev + 1):
        own_copy(k).start()

    @pl.when(outer)
    def _():
        own_copy(mdev + 1).start()

    pl.semaphore_wait(barrier, n - 1 + 9)

    def row_of(d, to, q, src):
        slot = slot_of(lax.rem(to, 2), q)
        row = jnp.clip(to * own - 1 + slot, 0, rows - 1)
        return rcopy(
            lat_hbm.at[:, row], x_ref.at[1, slot, pl.ds(mdev * src, mdev)],
            s_x.at[d, q], r_x.at[src, q], {"ens": to},
        )

    def goes(to, q):
        there = (to // 2) != xx
        exists = (q < last) | ((to // 2) != lax.rem(to, 2))
        return exists & ((q > 0) | jnp.logical_not(there))

    def edge_of(side, d, src):
        to = ens_at(d)
        return rcopy(
            leo.at[side, pl.ds(pl.multiple_of(to * own * mdev, 16), 32)], lei.at[1 - side, src],
            s_le.at[side, d], r_le.at[1 - side, src],
            {"ens": to, "space": left_s if side == 0 else right_s},
        )

    def send_rows(first, stop):
        @pl.loop(first, stop)
        def _(j):
            q = jnp.where(j < 3, lax.rem(j + 1, 3), j)
            for d in (2, 3, 1):
                to = ens_at(d)

                @pl.when(goes(to, q))
                def _():
                    row_of(d, to, q, e).start()

    send_rows(0, 3)
    lef32[...] = jnp.zeros_like(lef32)
    in_lat.wait()

    @pl.loop(0, rows)
    def _(row):
        for m in range(mdev):
            v = latv[m, row, 0:16].astype(F32)
            w = latv[m, row, cols - 16 : cols].astype(F32)
            lef32[0, pl.ds((1 + row) * mdev + m, 1)] = v[0:1]
            lef32[1, pl.ds((1 + row) * mdev + m, 1)] = w[15:16]

    leo[...] = lef32[...].astype(BF16)
    for d in (2, 3, 1, 0):
        for side in range(2):
            edge_of(side, d, e).start()
    send_rows(3, last + 1)

    @pl.when(jnp.logical_not(outer))
    def _():
        blank = jnp.zeros((members, cols, chans), BF16)
        slot = slot_of(core, last)
        x_ref[1, slot] = blank
        for c in range(3):
            sp[c, slot] = blank

    hand_slot = slot_of(core, 1)
    get_slot = slot_of(core, 0)
    theirs = pl.ds(2 * mdev * (1 - xx), 2 * mdev)
    hand = rcopy(
        x_ref.at[1, hand_slot, theirs], x_ref.at[1, last - get_slot, theirs],
        s_f.at[0], r_f.at[0], cpeer,
    )

    acc[...] = jnp.zeros_like(acc)
    lacc[...] = jnp.zeros_like(lacc)
    if pieces * span > TAPS * 128:
        tail = pl.ds(TAPS * 128, pieces * span - TAPS * 128)
        g[tail] = jnp.zeros((pieces * span - TAPS * 128, chans), F32)
        b2[tail] = jnp.zeros((pieces * span - TAPS * 128, chans), BF16)
    in_k.wait()
    in_t.wait()
    for k in range(mdev + 1):
        own_copy(k).wait()

    @pl.when(outer)
    def _():
        own_copy(mdev + 1).wait()

    for d in (0, 1, 2, 3):
        for side in range(2):
            edge_of(side, d, ens_at(d)).wait_recv()
    lef[...] = lei[...].astype(F32)

    col = lax.broadcasted_iota(jnp.int32, (cols, chans), 0)

    def shift(ref, slot, edge):
        for mem in range(members):
            v = ref[1, slot, mem].astype(F32)
            lo = jnp.where(col == 0, edge(0, mem), pltpu.roll(v, 1, 0))
            hi = jnp.where(col == cols - 1, edge(1, mem), pltpu.roll(v, cols - 1, 0))
            ref[0, slot, mem] = lo.astype(BF16)
            ref[2, slot, mem] = hi.astype(BF16)

    def ready(q):
        for d in range(1, 4):
            src = ens_at(d)
            there = (src // 2) != xx
            exists = ((q < last) | outer) & ((q > 0) | jnp.logical_not(there))

            @pl.when(exists)
            def _():
                row_of(d, e, q, src).wait_recv()

        @pl.when(q == 0)
        def _():
            hand.wait_recv()

        @pl.when(q == 1)
        def _():
            hand.start()

        slot = slot_of(core, q)
        shift(
            x_ref, slot,
            lambda side, mem: lef[side, mem // mdev, pl.ds(slot * mdev + mem % mdev, 1)],
        )

    def smooth(gap):
        square = gap * gap + smoothing * smoothing
        inv = lax.rsqrt(square)
        return gap * inv, square * inv

    def fields_of(i):
        total = None
        for a in range(3):
            for b in range(3):
                w = x_ref[b, i + a].reshape(cells, chans)
                term = jnp.dot(w, kv[a * 3 + b], preferred_element_type=F32)
                total = term if total is None else total + term
        fld[...] = total.reshape(members, cols, chans)

    def pairs_of(i):
        for blk in range(cols // 16):
            for lane in range(chans // 128):
                ln = pl.ds(lane * 128, 128)
                at = pl.ds(blk * 16, 16)
                tgt = tv[i, at, ln].astype(F32)
                f = [fld[m, at, ln] for m in range(members)]
                sums = [None] * members
                pair_w = None
                for m in range(members):
                    for o in range(m + 1, members):
                        sl, w = smooth(f[m] - f[o])
                        sums[m] = sl if sums[m] is None else sums[m] + sl
                        sums[o] = -sl if sums[o] is None else sums[o] - sl
                        pair_w = w if pair_w is None else pair_w + w
                own_w = None
                for m in range(members):
                    own_s, w = smooth(f[m] - tgt)
                    own_w = w if own_w is None else own_w + w
                    sl = own_s * (1.0 / members) - sums[m] * (1.0 / (members * (members - 1)))
                    sp[1, 1 + i, m, at, ln] = sl.astype(BF16)
                    if blk == 0:
                        eo[0, i, m : m + 1, ln] = sl[0:1]
                    if blk == cols // 16 - 1:
                        eo[1, i, m : m + 1, ln] = sl[15:16]
                lacc[:, ln] += own_w * (1.0 / members) - pair_w * (
                    1.0 / (members * (members - 1))
                )

    def rows_at(p, h, first=0, count=None):
        start = p * span + h * half + first
        return pl.ds(pl.multiple_of(start, 16), half if count is None else count)

    def by_core(tap):
        return rcopy(acc.at[1 - core, tap], r1.at[tap], s_c.at[tap], r_c.at[tap], cpeer)

    def by_y(p):
        there = rows_at(p, 1 - sy)
        return rcopy(b2.at[there], r2.at[there], s_y.at[p], r_y.at[p], ypeer)

    def y_here(p):
        here = rows_at(p, sy)
        return rcopy(b2.at[here], r2.at[here], s_y.at[p], r_y.at[p], ypeer)

    def z_rows(p, j, h=None):
        start = p * span + j * 2 * part + (0 if h is None else h * part)
        return pl.ds(pl.multiple_of(start, 16), 2 * part if h is None else part)

    def z_by_z(p, d, src):
        to = lax.rem(sz + d, nz)
        return rcopy(
            b2.at[z_rows(p, to)], rz.at[src, pl.ds(pl.multiple_of(p * 2 * part, 16), 2 * part)],
            s_z.at[p, d], r_z.at[p, src], {"space": to * 2 + sy},
        )

    def z_by_y(p, h):
        at = z_rows(p, sz, h)
        return rcopy(b2.at[at], r2.at[at], s_y.at[p], r_y.at[p], ypeer)

    def z_back_y(p, h):
        mine = gk_ref.at[core, z_rows(p, sz, h)]
        return rcopy(mine, mine, s_ay.at[p], r_ay.at[p], ypeer)

    def z_back_z(p, d, src):
        mine = gk_ref.at[core, z_rows(p, src)]
        to = lax.rem(sz + d, nz)
        return rcopy(mine, mine, s_az.at[p, d], r_az.at[p, src], {"space": to * 2 + sy})

    def z_back_core(p, c):
        mine = gk_ref.at[c, pl.ds(pl.multiple_of(p * span, 16), span)]
        return rcopy(mine, mine, s_ac.at[p, 0], r_ac.at[p, 0], cpeer)

    def core_sums():
        @pl.loop(0, TAPS)
        def _(tap):
            by_core(tap).wait_recv()
            v = (acc[core, tap] + r1[tap]).T
            at = pl.ds(pl.multiple_of(tap * 128, 128), 128)
            g[at] = v
            b2[at] = v.astype(BF16)
            ready_pieces = jnp.where(tap == TAPS - 1, pieces, (tap + 1) * 128 // span)

            @pl.when(ready_pieces > tap * 128 // span)
            def _():
                p = ready_pieces - 1

                @pl.when(p >= zfirst)
                def _():
                    by_y(p).start()

                if zfirst > 0:

                    @pl.when(p < zfirst)
                    def _():
                        @pl.loop(1, nz)
                        def _(d):
                            z_by_z(p, d, sz).start()


    def kernel_terms(start, stop, final):
        count = BLOCKS[0][1] - BLOCKS[0][0]
        i = jnp.where(core == 0, own - stop, start)

        for group, taps in enumerate(GROUPS):

            @pl.loop(0, count // 2)
            def _(k):
                at = pl.ds(pl.multiple_of(k * 2 * cells, 128), 2 * cells)
                if group == 0:
                    v = sp[1, pl.ds(1 + i + 2 * k, 2)].reshape(2 * cells, chans).astype(F32)
                    v = v.T.astype(BF16)
                    slt[:, at] = v
                else:
                    v = slt[:, at]
                for tap in taps:
                    a, b = tap // 3, tap % 3
                    w = x_ref[b, pl.ds(i + 2 * k + a, 2)].reshape(2 * cells, chans)
                    p = jnp.dot(v, w, preferred_element_type=F32)
                    for h in range(2):
                        acc[h, tap] += p[:, h * 128 : h * 128 + 128]

            @pl.when(final)
            def _():
                @pl.loop(taps[0], taps[-1] + 1)
                def _(tap):
                    by_core(tap).start()

    inner_halo = rcopy(
        sp.at[1, hand_slot], sp.at[1, last - get_slot], s_h.at[0], r_h.at[0], cpeer
    )
    outer_slot = slot_of(core, own)
    outer_halo = rcopy(
        sp.at[1, outer_slot], sp.at[1, last - slot_of(core, last)], s_h.at[1], r_h.at[1], across
    )
    edges = [
        rcopy(eb.at[1], eib.at[0], s_e.at[0], r_e.at[0], {"space": right_s}),
        rcopy(eb.at[0], eib.at[1], s_e.at[1], r_e.at[1], {"space": left_s}),
    ]

    @pl.loop(0, len(BLOCKS))
    def _(blk):
        start = jnp.int32(BLOCKS[0][0])
        stop = jnp.int32(BLOCKS[0][1])
        for k in range(1, len(BLOCKS)):
            start = jnp.where(blk == k, BLOCKS[k][0], start)
            stop = jnp.where(blk == k, BLOCKS[k][1], stop)
        first = jnp.where(blk == 0, 0, start + 2)

        @pl.loop(first, stop + 2)
        def _(t):
            ready(jnp.where(t < 3, lax.rem(t + 1, 3), t))

            @pl.when(t >= 2)
            def _():
                i = slot_of(core, t - 1) - 1
                fields_of(i)
                pairs_of(i)

            @pl.when(t == 2)
            def _():
                inner_halo.start()

            @pl.when(t == last)
            def _():
                eb[...] = eo[...].reshape(eb.shape).astype(BF16)
                for c in edges:
                    c.start()

                @pl.when(outer)
                def _():
                    outer_halo.start()

        kernel_terms(start, stop, blk == len(BLOCKS) - 1)

    core_sums()
    total = lacc[...]
    total = total[0:8, 0:128] + total[8:16, 0:128] + total[0:8, 128:256] + total[8:16, 128:256]
    l1[...] = total
    ls_core = rcopy(l1, lr1, s_ls.at[0], r_ls.at[0], cpeer)
    ls_core.start()
    ls_core.wait_recv()
    l2[...] = l1[...] + lr1[...]
    ls_x = rcopy(l2, lr2, s_ls.at[1], r_ls.at[1], xpeer)
    ls_x.start()

    hand_edge = rcopy(ei.at[:, hand_slot - 1], eh.at[0], s_h.at[2], r_h.at[2], cpeer)
    outer_edge = rcopy(ei.at[:, outer_slot - 1], eh.at[1], s_h.at[3], r_h.at[3], across)

    def slope_edges():
        for c in edges:
            c.wait_recv()
        ei[...] = eib[...].astype(F32).reshape(ei.shape)
        hand_edge.start()

        @pl.when(outer)
        def _():
            outer_edge.start()

        @pl.loop(0, own)
        def _(i):
            shift(sp, 1 + i, lambda side, mem: ei[side, i, mem : mem + 1])

        inner_halo.wait_recv()
        hand_edge.wait_recv()

    def by_z(p, d, src):
        to = lax.rem(sz + d, nz)
        return rcopy(
            b3.at[pl.ds(pl.multiple_of((p * nz + to) * part, 16), part)],
            r3.at[src, pl.ds(pl.multiple_of(p * part, 16), part)],
            s_z.at[p, d], r_z.at[p, src], {"space": to * 2 + sy},
        )

    def row_at(c, r):
        return jnp.where(c == 0, own - 2 - 2 * (r // 2), 2 * (r // 2)) + lax.rem(r, 2)

    def give(d, r):
        to, i = ens_at(d), row_at(core, r)
        return rcopy(
            gib.at[pl.ds(to * mdev, mdev), i], gi_ref.at[:, e * own + i],
            s_g.at[d, r], r_g.at[e, r], {"ens": to},
        )

    def taken(d, r):
        src = ens_at(d)
        i = row_at(lax.rem(src, 2), r)
        return rcopy(
            gib.at[pl.ds(e * mdev, mdev), i], gi_ref.at[:, src * own + i],
            s_g.at[d, r], r_g.at[src, r], {"ens": e},
        )

    def grad_in(pair):
        @pl.when((pair == 0) | ((pair == own // 2 - 1) & outer))
        def _():
            @pl.when(pair > 0)
            def _():
                outer_halo.wait_recv()
                outer_edge.wait_recv()

            k = jnp.where(pair == 0, 0, 1)
            shift(
                sp, slot_of(core, jnp.where(pair == 0, 0, last)),
                lambda side, mem: eh[k, side, mem : mem + 1],
            )

        i = base_of(pair)
        total = None
        for a in range(3):
            for b in range(3):
                w = sp[2 - b, pl.ds(i + 2 - a, 2)].reshape(2 * cells, chans)
                term = lax.dot_general(w, kv[a * 3 + b], NT, preferred_element_type=F32)
                total = term if total is None else total + term
        total = total.reshape(2, members, cols, chans).astype(BF16)
        for r in range(2):
            gib[:, i + r] = total[r]
        for m in range(mdev):
            gi_ref[m, pl.ds(e * own + i, 2)] = gib[e * mdev + m, pl.ds(i, 2)]

    def loss_to_strip(d, i):
        return rcopy(l3, lr3.at[i], s_lp.at[d], r_lp.at[i], {"space": lax.rem(s + d, n)})

    def by_x(p):
        at = pl.ds(pl.multiple_of(p * part, 16), part)
        return rcopy(b4.at[at], r4.at[at], s_v.at[p], r_v.at[p], xpeer)

    def back_z(p, d, src):
        mine = gk_ref.at[core, rows_at(p, sy, src * part, part)]
        to = lax.rem(sz + d, nz)
        return rcopy(mine, mine, s_az.at[p, d], r_az.at[p, src], {"space": to * 2 + sy})

    def back_y(p, h):
        mine = gk_ref.at[core, rows_at(p, h)]
        return rcopy(mine, mine, s_ay.at[p], r_ay.at[p], ypeer)

    def back_core(p, c, h, k):
        mine = gk_ref.at[c, rows_at(p, h)]
        return rcopy(mine, mine, s_ac.at[p, k], r_ac.at[p, k], cpeer)

    def step_y(p):
        y_here(p).wait_recv()
        here = rows_at(p, sy)
        total = g[here] + r2[here].astype(F32)
        g[here] = total
        b3[pl.ds(pl.multiple_of(p * half, 16), half)] = total.astype(BF16)

        @pl.loop(1, nz)
        def _(d):
            by_z(p, d, sz).start()

    def step_z(p):
        def take(d, v):
            src = lax.rem(sz + d, nz)
            by_z(p, d, src).wait_recv()
            return v + r3[src, pl.ds(pl.multiple_of(p * part, 16), part)].astype(F32)

        v = lax.fori_loop(1, nz, take, g[rows_at(p, sy, sz * part, part)])
        b4[pl.ds(pl.multiple_of(p * part, 16), part)] = v.astype(BF16)
        by_x(p).start()

    def step_x(p):
        by_x(p).wait_recv()
        at = pl.ds(pl.multiple_of(p * part, 16), part)
        v = b4[at].astype(F32) + r4[at].astype(F32)
        gk_ref[core, rows_at(p, sy, sz * part, part)] = v.astype(BF16)

        @pl.loop(1, nz)
        def _(d):
            back_z(p, d, sz).start()

    def step_back_z(p):
        @pl.loop(1, nz)
        def _(d):
            back_z(p, d, lax.rem(sz + d, nz)).wait_recv()

        back_y(p, sy).start()
        back_core(p, core, sy, 0).start()

    def step_back_y(p):
        back_y(p, 1 - sy).wait_recv()
        back_core(p, core, 1 - sy, 1).start()

    def z_step_z(p):
        at = z_rows(p, sz)

        def take(d, v):
            src = lax.rem(sz + d, nz)
            z_by_z(p, d, src).wait_recv()
            return v + rz[src, pl.ds(pl.multiple_of(p * 2 * part, 16), 2 * part)].astype(F32)

        v = lax.fori_loop(1, nz, take, g[at])
        g[at] = v
        b2[at] = v.astype(BF16)
        z_by_y(p, 1 - sy).start()

    def z_step_y(p):
        z_by_y(p, sy).wait_recv()
        at = z_rows(p, sz, sy)
        v = g[at] + r2[at].astype(F32)
        b4[pl.ds(pl.multiple_of(p * part, 16), part)] = v.astype(BF16)
        by_x(p).start()

    def z_step_x(p):
        by_x(p).wait_recv()
        at = pl.ds(pl.multiple_of(p * part, 16), part)
        v = b4[at].astype(F32) + r4[at].astype(F32)
        gk_ref[core, z_rows(p, sz, sy)] = v.astype(BF16)
        z_back_y(p, sy).start()

    def z_step_back_y(p):
        z_back_y(p, 1 - sy).wait_recv()

        @pl.loop(1, nz)
        def _(d):
            z_back_z(p, d, sz).start()

    def z_step_back_z(p):
        @pl.loop(1, nz)
        def _(d):
            z_back_z(p, d, lax.rem(sz + d, nz)).wait_recv()

        z_back_core(p, core).start()

    early = ((step_y, -zfirst), (step_z, 5 - zfirst))
    late = early + ((step_x, 8 - zfirst), (step_back_z, 13 - zfirst), (step_back_y, 17 - zfirst))
    z_early = ((z_step_z, ZLAG[0]),)
    z_late = tuple(zip((z_step_y, z_step_x, z_step_back_y, z_step_back_z), ZLAG[1:]))
    sent = 5 - zfirst + pieces

    def step(t, stages, z_stages):
        for stage, lag in stages:
            p = t - lag

            @pl.when((p >= zfirst) & (p < pieces))
            def _():
                stage(p)

        if zfirst > 0:
            for stage, lag in z_stages:
                p = t - lag

                @pl.when((p >= 0) & (p < zfirst))
                def _():
                    stage(p)

    def give_row(r):
        for d in (2, 3, 1):
            give(d, r).start()

    slope_edges()

    @pl.loop(0, own // 2)
    def _(pair):
        grad_in(pair)

        @pl.loop(jnp.minimum(2 * pair, EARLY), jnp.minimum(2 * pair + 2, EARLY))
        def _(r):
            give_row(r)

        @pl.loop(2 * pair, 2 * pair + 2)
        def _(t):
            step(t, early, z_early)

    @pl.loop(own, max(late[-1][1] + pieces, ZLAG[-1] + zfirst))
    def _(t):
        r = EARLY + (t - LATE_AT) // LATE_STEP

        @pl.when((t >= LATE_AT) & (lax.rem(t - LATE_AT, LATE_STEP) == 0) & (r < own))
        def _():
            give_row(r)

        step(t, late, z_late)

        @pl.when(t == sent)
        def _():
            ls_x.wait_recv()
            l3[...] = l2[...] + lr2[...]

            @pl.loop(1, n)
            def _(d):
                loss_to_strip(d, s).start()

    def take_loss(d, v):
        i = lax.rem(s + d, n)
        loss_to_strip(d, i).wait_recv()
        return v + lr3[i]

    loss_ref[...] = lax.fori_loop(1, n, take_loss, l3[...])

    @pl.loop(0, own)
    def _(r):
        for d in range(1, 4):
            give(d, r).wait_send()
            taken(d, r).wait_recv()

    @pl.loop(0, pieces)
    def _(p):
        @pl.when(p >= zfirst)
        def _():
            back_core(p, 1 - core, sy, 0).wait_recv()
            back_core(p, 1 - core, 1 - sy, 1).wait_recv()

        if zfirst > 0:

            @pl.when(p < zfirst)
            def _():
                z_back_core(p, 1 - core).wait_recv()

    @pl.loop(0, last + 1)
    def _(q):
        for d in range(1, 4):
            to = ens_at(d)

            @pl.when(goes(to, q))
            def _():
                row_of(d, to, q, e).wait_send()

    for d in range(4):
        for side in range(2):
            edge_of(side, d, e).wait_send()

    @pl.when(outer)
    def _():
        outer_halo.wait_send()
        outer_edge.wait_send()

    @pl.loop(1, n)
    def _(d):
        loss_to_strip(d, s).wait_send()

    @pl.loop(0, pieces)
    def _(p):
        by_x(p).wait_send()

        @pl.when(p >= zfirst)
        def _():
            by_y(p).wait_send()
            back_y(p, sy).wait_send()
            back_core(p, core, sy, 0).wait_send()
            back_core(p, core, 1 - sy, 1).wait_send()

            @pl.loop(1, nz)
            def _(d):
                by_z(p, d, sz).wait_send()
                back_z(p, d, sz).wait_send()

        if zfirst > 0:

            @pl.when(p < zfirst)
            def _():
                z_by_y(p, 1 - sy).wait_send()
                z_back_y(p, sy).wait_send()
                z_back_core(p, core).wait_send()

                @pl.loop(1, nz)
                def _(d):
                    z_by_z(p, d, sz).wait_send()
                    z_back_z(p, d, sz).wait_send()

    @pl.loop(0, TAPS)
    def _(tap):
        by_core(tap).wait_send()

    for c in edges + [hand, inner_halo, hand_edge, ls_core, ls_x]:
        c.wait_send()


def finish(scale, loss_scale, gi_ref, gk_ref, l_ref, gi_out, gk_out, loss_out, wide, sem):
    taps = wide.shape[0]
    out_gi = pltpu.make_async_copy(gi_ref, gi_out, sem.at[taps])
    out_gi.start()

    def out_tap(tap):
        return pltpu.make_async_copy(wide.at[tap], gk_out.at[tap], sem.at[tap])

    for tap in range(taps):
        for h in range(2):
            v = gk_ref[h, tap * 128 : tap * 128 + 128].astype(F32)
            wide[tap, h * 128 : h * 128 + 128] = v * scale
        out_tap(tap).start()
    loss_out[0, 0] = jnp.sum(l_ref[...]) * loss_scale
    for tap in range(taps):
        out_tap(tap).wait()
    out_gi.wait()


def local(n, latents, targets, kernel):
    mdev, rows, cols, chans = latents.shape
    members = mdev * 4
    own = rows // 4
    slots = own + 2
    cells = members * cols
    pieces, part = pieces_of(n)
    nz = n // 2
    hp = pieces * part * n
    vmem, dma = pltpu.VMEM, pltpu.SemaphoreType.DMA
    hbm = pl.BlockSpec(memory_space=pltpu.HBM)
    on_chip = pl.BlockSpec(memory_space=vmem)
    shifted = vmem((3, slots, members, cols, chans), BF16)
    edge = vmem((2, own, members, chans), F32)
    tile = vmem((8, 128), F32)
    edge_rows = -(-((rows - own) * mdev + 32) // 16) * 16
    gi, gk, loss = pl.pallas_call(
        functools.partial(body, n, members),
        name="crps_step",
        out_shape=(
            vmem(latents.shape, BF16),
            vmem((2, hp, chans), BF16),
            vmem((8, 128), F32),
        ),
        in_specs=[hbm] * 3,
        out_specs=(on_chip,) * 3,
        scratch_shapes=[
            shifted,
            vmem((mdev, rows, cols, chans), BF16),
            vmem((own, cols, chans), BF16),
            vmem((TAPS, chans, chans), BF16),
            vmem((2, edge_rows, chans), F32),
            vmem((2, edge_rows, chans), BF16),
            vmem((2, 4, 32, chans), BF16),
            vmem((2, 4, 32, chans), F32),
            vmem((members, cols, chans), F32),
            shifted,
            vmem((2, TAPS, chans, 128), F32),
            edge,
            vmem((2, own * members, chans), BF16),
            vmem((2, own * members, chans), BF16),
            edge,
            vmem((2, 2, members, chans), F32),
            vmem((members, own, cols, chans), BF16),
            vmem((16, chans), F32),
            vmem((chans, (BLOCKS[0][1] - BLOCKS[0][0]) * cells), BF16),
            vmem((TAPS, chans, 128), F32),
            vmem((hp, chans), F32),
            vmem((hp, chans), BF16),
            vmem((hp, chans), BF16),
            vmem((hp // 2, chans), BF16),
            vmem((nz, pieces * part, chans), BF16),
            vmem((nz, max(first_by_z(n), 1) * 2 * part, chans), BF16),
            vmem((pieces * part, chans), BF16),
            vmem((pieces * part, chans), BF16),
            tile, tile, tile, tile, tile,
            vmem((n, 8, 128), F32),
            dma((3,)), dma((mdev + 2,)),
            dma((4, slots)), dma((4, slots)), dma((1,)), dma((1,)),
            dma((2, 4)), dma((2, 4)), dma((2,)), dma((2,)), dma((4,)), dma((4,)),
            dma((4, own)), dma((4, own)),
            dma((TAPS,)), dma((TAPS,)), dma((pieces,)), dma((pieces,)),
            dma((pieces, nz)), dma((pieces, nz)), dma((pieces,)), dma((pieces,)),
            dma((pieces, nz)), dma((pieces, nz)), dma((pieces,)), dma((pieces,)),
            dma((pieces, 2)), dma((pieces, 2)),
            dma((2,)), dma((2,)), dma((n,)), dma((n,)),
        ],
        compiler_params=pltpu.CompilerParams(
            collective_id=0, has_side_effects=True, vmem_limit_bytes=56 * 2**20
        ),
    )(latents, targets, kernel.reshape(TAPS, chans, chans))
    longitude = cols * n
    gi, gk, loss = pl.pallas_call(
        functools.partial(
            finish, 1.0 / (members * rows * longitude), 1.0 / (rows * longitude * chans)
        ),
        name="finish",
        out_shape=(
            jax.ShapeDtypeStruct(latents.shape, BF16),
            jax.ShapeDtypeStruct((TAPS, chans, chans), F32),
            jax.ShapeDtypeStruct((1, 1), F32),
        ),
        in_specs=[on_chip] * 3,
        out_specs=(hbm, hbm, pl.BlockSpec(memory_space=pltpu.SMEM)),
        scratch_shapes=[vmem((TAPS, chans, chans), F32), dma((TAPS + 1,))],
        compiler_params=pltpu.CompilerParams(vmem_limit_bytes=24 * 2**20),
    )(gi, gk, loss)
    return loss.reshape(()), gi, gk.reshape(3, 3, chans, chans)


def solution(mesh):
    in_specs = (P("ens", None, "space", None), P(None, "space", None), P())
    out_specs = (P(), P("ens", None, "space", None), P())
    return jax.shard_map(
        functools.partial(local, mesh.shape["space"]),
        mesh=mesh, in_specs=in_specs, out_specs=out_specs, check_vma=False,
    )
```

```python
import functools

import jax
import jax.numpy as jnp
from jax import lax
from jax.experimental import pallas as pl
from jax.experimental.pallas import tpu as pltpu
from jax.sharding import PartitionSpec as P

smoothing = 0.1
F32, BF16 = jnp.float32, jnp.bfloat16
NT = (((1,), (1,)), ((), ()))
TAPS = 9
EARLY, LATE_AT, LATE_STEP = 2, 12, 1
BLOCKS = ((0, 4), (4, 8))
ZFIRST = 3
ZLAG = (3, 8, 11, 15, 18)
GROUPS = ((0, 1, 2, 3, 4), (5, 6, 7, 8))


def pieces_of(n):
    units = -(-TAPS * 128 // (16 * n))
    pieces = min(TAPS, units)
    return pieces, 16 * -(-units // pieces)


def first_by_z(n):
    return ZFIRST if pieces_of(n)[0] == TAPS else 0


def body(
    n, members,
    lat_hbm, t_hbm, k_hbm,
    gi_ref, gk_ref, loss_ref,
    x_ref, latv, tv, kv, lef32, leo, lei, lef, fld, sp, acc, eo, eb, eib, ei, eh, gib, lacc, slt,
    r1, g, b2, r2, b3, r3, rz, b4, r4, l1, lr1, l2, lr2, l3, lr3,
    s_in, s_own, s_x, r_x, s_f, r_f, s_le, r_le, s_e, r_e, s_h, r_h, s_g, r_g,
    s_c, r_c, s_y, r_y, s_z, r_z, s_v, r_v, s_az, r_az, s_ay, r_ay, s_ac, r_ac,
    s_ls, r_ls, s_lp, r_lp,
):
    mdev, rows, cols, chans = lat_hbm.shape
    own = rows // 4
    last = own + 1
    cells = members * cols
    pieces, part = pieces_of(n)
    nz = n // 2
    zfirst = first_by_z(n)
    half = part * nz
    span = 2 * half
    e = lax.axis_index("ens")
    s = lax.axis_index("space")
    core = lax.rem(e, 2)
    xx = e // 2
    sy = lax.rem(s, 2)
    sz = s // 2
    outer = xx != core
    cpeer = {"ens": xx * 2 + (1 - core)}
    xpeer = {"ens": (1 - xx) * 2 + core}
    across = {"ens": 3 - e}
    ypeer = {"space": sz * 2 + (1 - sy)}
    right_s = lax.rem(s + 1, n)
    left_s = lax.rem(s + n - 1, n)
    MESH = pl.DeviceIdType.MESH

    def rcopy(src, dst, ss, rs, dev):
        return pltpu.make_async_remote_copy(
            src_ref=src, dst_ref=dst, send_sem=ss, recv_sem=rs,
            device_id=dev, device_id_type=MESH,
        )

    def ens_at(d):
        return lax.rem(e + d, 4)

    def slot_of(c, q):
        return jnp.where(c == 0, last - q, q)

    def base_of(pair):
        return jnp.where(core == 0, own - 2 - 2 * pair, 2 * pair)

    in_lat = pltpu.make_async_copy(lat_hbm, latv, s_in.at[0])
    in_k = pltpu.make_async_copy(k_hbm, kv, s_in.at[1])
    in_t = pltpu.make_async_copy(t_hbm.at[pl.ds(e * own, own)], tv, s_in.at[2])
    in_lat.start()
    in_k.start()
    in_t.start()
    barrier = pltpu.get_barrier_semaphore()
    for d in range(1, 4):
        for strip in (s, right_s, left_s):
            pl.semaphore_signal(
                barrier, inc=1, device_id={"ens": ens_at(d), "space": strip}, device_id_type=MESH
            )

    @pl.loop(1, n)
    def _(d):
        pl.semaphore_signal(
            barrier, inc=1, device_id={"space": lax.rem(s + d, n)}, device_id_type=MESH
        )

    def own_copy(k):
        if k < mdev:
            return pltpu.make_async_copy(
                lat_hbm.at[k, pl.ds(e * own, own)], x_ref.at[1, pl.ds(1, own), e * mdev + k],
                s_own.at[k],
            )
        slot = slot_of(core, 0 if k == mdev else last)
        row = jnp.clip(e * own - 1 + slot, 0, rows - 1)
        return pltpu.make_async_copy(
            lat_hbm.at[:, row], x_ref.at[1, slot, pl.ds(e * mdev, mdev)], s_own.at[k]
        )

    for k in range(mdev + 1):
        own_copy(k).start()

    @pl.when(outer)
    def _():
        own_copy(mdev + 1).start()

    pl.semaphore_wait(barrier, n - 1 + 9)

    def row_of(d, to, q, src):
        slot = slot_of(lax.rem(to, 2), q)
        row = jnp.clip(to * own - 1 + slot, 0, rows - 1)
        return rcopy(
            lat_hbm.at[:, row], x_ref.at[1, slot, pl.ds(mdev * src, mdev)],
            s_x.at[d, q], r_x.at[src, q], {"ens": to},
        )

    def goes(to, q):
        there = (to // 2) != xx
        exists = (q < last) | ((to // 2) != lax.rem(to, 2))
        return exists & ((q > 0) | jnp.logical_not(there))

    def edge_of(side, d, src):
        to = ens_at(d)
        return rcopy(
            leo.at[side, pl.ds(pl.multiple_of(to * own * mdev, 16), 32)], lei.at[1 - side, src],
            s_le.at[side, d], r_le.at[1 - side, src],
            {"ens": to, "space": left_s if side == 0 else right_s},
        )

    def send_rows(first, stop):
        @pl.loop(first, stop)
        def _(j):
            q = jnp.where(j < 3, lax.rem(j + 1, 3), j)
            for d in (2, 3, 1):
                to = ens_at(d)

                @pl.when(goes(to, q))
                def _():
                    row_of(d, to, q, e).start()

    send_rows(0, 3)
    lef32[...] = jnp.zeros_like(lef32)
    in_lat.wait()

    @pl.loop(0, rows)
    def _(row):
        for m in range(mdev):
            v = latv[m, row, 0:16].astype(F32)
            w = latv[m, row, cols - 16 : cols].astype(F32)
            lef32[0, pl.ds((1 + row) * mdev + m, 1)] = v[0:1]
            lef32[1, pl.ds((1 + row) * mdev + m, 1)] = w[15:16]

    leo[...] = lef32[...].astype(BF16)
    for d in (2, 3, 1, 0):
        for side in range(2):
            edge_of(side, d, e).start()
    send_rows(3, last + 1)

    @pl.when(jnp.logical_not(outer))
    def _():
        blank = jnp.zeros((members, cols, chans), BF16)
        slot = slot_of(core, last)
        x_ref[1, slot] = blank
        for c in range(3):
            sp[c, slot] = blank

    hand_slot = slot_of(core, 1)
    get_slot = slot_of(core, 0)
    theirs = pl.ds(2 * mdev * (1 - xx), 2 * mdev)
    hand = rcopy(
        x_ref.at[1, hand_slot, theirs], x_ref.at[1, last - get_slot, theirs],
        s_f.at[0], r_f.at[0], cpeer,
    )

    acc[...] = jnp.zeros_like(acc)
    lacc[...] = jnp.zeros_like(lacc)
    if pieces * span > TAPS * 128:
        tail = pl.ds(TAPS * 128, pieces * span - TAPS * 128)
        g[tail] = jnp.zeros((pieces * span - TAPS * 128, chans), F32)
        b2[tail] = jnp.zeros((pieces * span - TAPS * 128, chans), BF16)
    in_k.wait()
    in_t.wait()
    for k in range(mdev + 1):
        own_copy(k).wait()

    @pl.when(outer)
    def _():
        own_copy(mdev + 1).wait()

    for d in (0, 1, 2, 3):
        for side in range(2):
            edge_of(side, d, ens_at(d)).wait_recv()
    lef[...] = lei[...].astype(F32)

    col = lax.broadcasted_iota(jnp.int32, (cols, chans), 0)

    def shift(ref, slot, edge):
        for mem in range(members):
            v = ref[1, slot, mem].astype(F32)
            lo = jnp.where(col == 0, edge(0, mem), pltpu.roll(v, 1, 0))
            hi = jnp.where(col == cols - 1, edge(1, mem), pltpu.roll(v, cols - 1, 0))
            ref[0, slot, mem] = lo.astype(BF16)
            ref[2, slot, mem] = hi.astype(BF16)

    def ready(q):
        for d in range(1, 4):
            src = ens_at(d)
            there = (src // 2) != xx
            exists = ((q < last) | outer) & ((q > 0) | jnp.logical_not(there))

            @pl.when(exists)
            def _():
                row_of(d, e, q, src).wait_recv()

        @pl.when(q == 0)
        def _():
            hand.wait_recv()

        @pl.when(q == 1)
        def _():
            hand.start()

        slot = slot_of(core, q)
        shift(
            x_ref, slot,
            lambda side, mem: lef[side, mem // mdev, pl.ds(slot * mdev + mem % mdev, 1)],
        )

    def smooth(gap):
        square = gap * gap + smoothing * smoothing
        inv = lax.rsqrt(square)
        return gap * inv, square * inv

    def fields_of(i):
        total = None
        for a in range(3):
            for b in range(3):
                w = x_ref[b, i + a].reshape(cells, chans)
                term = jnp.dot(w, kv[a * 3 + b], preferred_element_type=F32)
                total = term if total is None else total + term
        fld[...] = total.reshape(members, cols, chans)

    def pairs_of(i):
        for blk in range(cols // 16):
            for lane in range(chans // 128):
                ln = pl.ds(lane * 128, 128)
                at = pl.ds(blk * 16, 16)
                tgt = tv[i, at, ln].astype(F32)
                f = [fld[m, at, ln] for m in range(members)]
                sums = [None] * members
                pair_w = None
                for m in range(members):
                    for o in range(m + 1, members):
                        sl, w = smooth(f[m] - f[o])
                        sums[m] = sl if sums[m] is None else sums[m] + sl
                        sums[o] = -sl if sums[o] is None else sums[o] - sl
                        pair_w = w if pair_w is None else pair_w + w
                own_w = None
                for m in range(members):
                    own_s, w = smooth(f[m] - tgt)
                    own_w = w if own_w is None else own_w + w
                    sl = own_s * (1.0 / members) - sums[m] * (1.0 / (members * (members - 1)))
                    sp[1, 1 + i, m, at, ln] = sl.astype(BF16)
                    if blk == 0:
                        eo[0, i, m : m + 1, ln] = sl[0:1]
                    if blk == cols // 16 - 1:
                        eo[1, i, m : m + 1, ln] = sl[15:16]
                lacc[:, ln] += own_w * (1.0 / members) - pair_w * (
                    1.0 / (members * (members - 1))
                )

    def rows_at(p, h, first=0, count=None):
        start = p * span + h * half + first
        return pl.ds(pl.multiple_of(start, 16), half if count is None else count)

    def by_core(tap):
        return rcopy(acc.at[1 - core, tap], r1.at[tap], s_c.at[tap], r_c.at[tap], cpeer)

    def by_y(p):
        there = rows_at(p, 1 - sy)
        return rcopy(b2.at[there], r2.at[there], s_y.at[p], r_y.at[p], ypeer)

    def y_here(p):
        here = rows_at(p, sy)
        return rcopy(b2.at[here], r2.at[here], s_y.at[p], r_y.at[p], ypeer)

    def z_rows(p, j, h=None):
        start = p * span + j * 2 * part + (0 if h is None else h * part)
        return pl.ds(pl.multiple_of(start, 16), 2 * part if h is None else part)

    def z_by_z(p, d, src):
        to = lax.rem(sz + d, nz)
        return rcopy(
            b2.at[z_rows(p, to)], rz.at[src, pl.ds(pl.multiple_of(p * 2 * part, 16), 2 * part)],
            s_z.at[p, d], r_z.at[p, src], {"space": to * 2 + sy},
        )

    def z_by_y(p, h):
        at = z_rows(p, sz, h)
        return rcopy(b2.at[at], r2.at[at], s_y.at[p], r_y.at[p], ypeer)

    def z_back_y(p, h):
        mine = gk_ref.at[core, z_rows(p, sz, h)]
        return rcopy(mine, mine, s_ay.at[p], r_ay.at[p], ypeer)

    def z_back_z(p, d, src):
        mine = gk_ref.at[core, z_rows(p, src)]
        to = lax.rem(sz + d, nz)
        return rcopy(mine, mine, s_az.at[p, d], r_az.at[p, src], {"space": to * 2 + sy})

    def z_back_core(p, c):
        mine = gk_ref.at[c, pl.ds(pl.multiple_of(p * span, 16), span)]
        return rcopy(mine, mine, s_ac.at[p, 0], r_ac.at[p, 0], cpeer)

    def core_sums():
        @pl.loop(0, TAPS)
        def _(tap):
            by_core(tap).wait_recv()
            v = (acc[core, tap] + r1[tap]).T
            at = pl.ds(pl.multiple_of(tap * 128, 128), 128)
            g[at] = v
            b2[at] = v.astype(BF16)
            ready_pieces = jnp.where(tap == TAPS - 1, pieces, (tap + 1) * 128 // span)

            @pl.when(ready_pieces > tap * 128 // span)
            def _():
                p = ready_pieces - 1

                @pl.when(p >= zfirst)
                def _():
                    by_y(p).start()

                if zfirst > 0:

                    @pl.when(p < zfirst)
                    def _():
                        @pl.loop(1, nz)
                        def _(d):
                            z_by_z(p, d, sz).start()


    def kernel_terms(start, stop, final):
        count = BLOCKS[0][1] - BLOCKS[0][0]
        i = jnp.where(core == 0, own - stop, start)

        for group, taps in enumerate(GROUPS):

            @pl.loop(0, count // 2)
            def _(k):
                at = pl.ds(pl.multiple_of(k * 2 * cells, 128), 2 * cells)
                if group == 0:
                    v = sp[1, pl.ds(1 + i + 2 * k, 2)].reshape(2 * cells, chans).astype(F32)
                    v = v.T.astype(BF16)
                    slt[:, at] = v
                else:
                    v = slt[:, at]
                for tap in taps:
                    a, b = tap // 3, tap % 3
                    w = x_ref[b, pl.ds(i + 2 * k + a, 2)].reshape(2 * cells, chans)
                    p = jnp.dot(v, w, preferred_element_type=F32)
                    for h in range(2):
                        acc[h, tap] += p[:, h * 128 : h * 128 + 128]

            @pl.when(final)
            def _():
                @pl.loop(taps[0], taps[-1] + 1)
                def _(tap):
                    by_core(tap).start()

    inner_halo = rcopy(
        sp.at[1, hand_slot], sp.at[1, last - get_slot], s_h.at[0], r_h.at[0], cpeer
    )
    outer_slot = slot_of(core, own)
    outer_halo = rcopy(
        sp.at[1, outer_slot], sp.at[1, last - slot_of(core, last)], s_h.at[1], r_h.at[1], across
    )
    edges = [
        rcopy(eb.at[1], eib.at[0], s_e.at[0], r_e.at[0], {"space": right_s}),
        rcopy(eb.at[0], eib.at[1], s_e.at[1], r_e.at[1], {"space": left_s}),
    ]

    @pl.loop(0, len(BLOCKS))
    def _(blk):
        start = jnp.int32(BLOCKS[0][0])
        stop = jnp.int32(BLOCKS[0][1])
        for k in range(1, len(BLOCKS)):
            start = jnp.where(blk == k, BLOCKS[k][0], start)
            stop = jnp.where(blk == k, BLOCKS[k][1], stop)
        first = jnp.where(blk == 0, 0, start + 2)

        @pl.loop(first, stop + 2)
        def _(t):
            ready(jnp.where(t < 3, lax.rem(t + 1, 3), t))

            @pl.when(t >= 2)
            def _():
                i = slot_of(core, t - 1) - 1
                fields_of(i)
                pairs_of(i)

            @pl.when(t == 2)
            def _():
                inner_halo.start()

            @pl.when(t == last)
            def _():
                eb[...] = eo[...].reshape(eb.shape).astype(BF16)
                for c in edges:
                    c.start()

                @pl.when(outer)
                def _():
                    outer_halo.start()

        kernel_terms(start, stop, blk == len(BLOCKS) - 1)

    core_sums()
    total = lacc[...]
    total = total[0:8, 0:128] + total[8:16, 0:128] + total[0:8, 128:256] + total[8:16, 128:256]
    l1[...] = total
    ls_core = rcopy(l1, lr1, s_ls.at[0], r_ls.at[0], cpeer)
    ls_core.start()
    ls_core.wait_recv()
    l2[...] = l1[...] + lr1[...]
    ls_x = rcopy(l2, lr2, s_ls.at[1], r_ls.at[1], xpeer)
    ls_x.start()

    hand_edge = rcopy(ei.at[:, hand_slot - 1], eh.at[0], s_h.at[2], r_h.at[2], cpeer)
    outer_edge = rcopy(ei.at[:, outer_slot - 1], eh.at[1], s_h.at[3], r_h.at[3], across)

    def slope_edges():
        for c in edges:
            c.wait_recv()
        ei[...] = eib[...].astype(F32).reshape(ei.shape)
        hand_edge.start()

        @pl.when(outer)
        def _():
            outer_edge.start()

        @pl.loop(0, own)
        def _(i):
            shift(sp, 1 + i, lambda side, mem: ei[side, i, mem : mem + 1])

        inner_halo.wait_recv()
        hand_edge.wait_recv()

    def by_z(p, d, src):
        to = lax.rem(sz + d, nz)
        return rcopy(
            b3.at[pl.ds(pl.multiple_of((p * nz + to) * part, 16), part)],
            r3.at[src, pl.ds(pl.multiple_of(p * part, 16), part)],
            s_z.at[p, d], r_z.at[p, src], {"space": to * 2 + sy},
        )

    def row_at(c, r):
        return jnp.where(c == 0, own - 2 - 2 * (r // 2), 2 * (r // 2)) + lax.rem(r, 2)

    def give(d, r):
        to, i = ens_at(d), row_at(core, r)
        return rcopy(
            gib.at[pl.ds(to * mdev, mdev), i], gi_ref.at[:, e * own + i],
            s_g.at[d, r], r_g.at[e, r], {"ens": to},
        )

    def taken(d, r):
        src = ens_at(d)
        i = row_at(lax.rem(src, 2), r)
        return rcopy(
            gib.at[pl.ds(e * mdev, mdev), i], gi_ref.at[:, src * own + i],
            s_g.at[d, r], r_g.at[src, r], {"ens": e},
        )

    def grad_in(pair):
        @pl.when((pair == 0) | ((pair == own // 2 - 1) & outer))
        def _():
            @pl.when(pair > 0)
            def _():
                outer_halo.wait_recv()
                outer_edge.wait_recv()

            k = jnp.where(pair == 0, 0, 1)
            shift(
                sp, slot_of(core, jnp.where(pair == 0, 0, last)),
                lambda side, mem: eh[k, side, mem : mem + 1],
            )

        i = base_of(pair)
        total = None
        for a in range(3):
            for b in range(3):
                w = sp[2 - b, pl.ds(i + 2 - a, 2)].reshape(2 * cells, chans)
                term = lax.dot_general(w, kv[a * 3 + b], NT, preferred_element_type=F32)
                total = term if total is None else total + term
        total = total.reshape(2, members, cols, chans).astype(BF16)
        for r in range(2):
            gib[:, i + r] = total[r]
        for m in range(mdev):
            gi_ref[m, pl.ds(e * own + i, 2)] = gib[e * mdev + m, pl.ds(i, 2)]

    def loss_to_strip(d, i):
        return rcopy(l3, lr3.at[i], s_lp.at[d], r_lp.at[i], {"space": lax.rem(s + d, n)})

    def by_x(p):
        at = pl.ds(pl.multiple_of(p * part, 16), part)
        return rcopy(b4.at[at], r4.at[at], s_v.at[p], r_v.at[p], xpeer)

    def back_z(p, d, src):
        mine = gk_ref.at[core, rows_at(p, sy, src * part, part)]
        to = lax.rem(sz + d, nz)
        return rcopy(mine, mine, s_az.at[p, d], r_az.at[p, src], {"space": to * 2 + sy})

    def back_y(p, h):
        mine = gk_ref.at[core, rows_at(p, h)]
        return rcopy(mine, mine, s_ay.at[p], r_ay.at[p], ypeer)

    def back_core(p, c, h, k):
        mine = gk_ref.at[c, rows_at(p, h)]
        return rcopy(mine, mine, s_ac.at[p, k], r_ac.at[p, k], cpeer)

    def step_y(p):
        y_here(p).wait_recv()
        here = rows_at(p, sy)
        total = g[here] + r2[here].astype(F32)
        g[here] = total
        b3[pl.ds(pl.multiple_of(p * half, 16), half)] = total.astype(BF16)

        @pl.loop(1, nz)
        def _(d):
            by_z(p, d, sz).start()

    def step_z(p):
        def take(d, v):
            src = lax.rem(sz + d, nz)
            by_z(p, d, src).wait_recv()
            return v + r3[src, pl.ds(pl.multiple_of(p * part, 16), part)].astype(F32)

        v = lax.fori_loop(1, nz, take, g[rows_at(p, sy, sz * part, part)])
        b4[pl.ds(pl.multiple_of(p * part, 16), part)] = v.astype(BF16)
        by_x(p).start()

    def step_x(p):
        by_x(p).wait_recv()
        at = pl.ds(pl.multiple_of(p * part, 16), part)
        v = b4[at].astype(F32) + r4[at].astype(F32)
        gk_ref[core, rows_at(p, sy, sz * part, part)] = v.astype(BF16)

        @pl.loop(1, nz)
        def _(d):
            back_z(p, d, sz).start()

    def step_back_z(p):
        @pl.loop(1, nz)
        def _(d):
            back_z(p, d, lax.rem(sz + d, nz)).wait_recv()

        back_y(p, sy).start()
        back_core(p, core, sy, 0).start()

    def step_back_y(p):
        back_y(p, 1 - sy).wait_recv()
        back_core(p, core, 1 - sy, 1).start()

    def z_step_z(p):
        at = z_rows(p, sz)

        def take(d, v):
            src = lax.rem(sz + d, nz)
            z_by_z(p, d, src).wait_recv()
            return v + rz[src, pl.ds(pl.multiple_of(p * 2 * part, 16), 2 * part)].astype(F32)

        v = lax.fori_loop(1, nz, take, g[at])
        g[at] = v
        b2[at] = v.astype(BF16)
        z_by_y(p, 1 - sy).start()

    def z_step_y(p):
        z_by_y(p, sy).wait_recv()
        at = z_rows(p, sz, sy)
        v = g[at] + r2[at].astype(F32)
        b4[pl.ds(pl.multiple_of(p * part, 16), part)] = v.astype(BF16)
        by_x(p).start()

    def z_step_x(p):
        by_x(p).wait_recv()
        at = pl.ds(pl.multiple_of(p * part, 16), part)
        v = b4[at].astype(F32) + r4[at].astype(F32)
        gk_ref[core, z_rows(p, sz, sy)] = v.astype(BF16)
        z_back_y(p, sy).start()

    def z_step_back_y(p):
        z_back_y(p, 1 - sy).wait_recv()

        @pl.loop(1, nz)
        def _(d):
            z_back_z(p, d, sz).start()

    def z_step_back_z(p):
        @pl.loop(1, nz)
        def _(d):
            z_back_z(p, d, lax.rem(sz + d, nz)).wait_recv()

        z_back_core(p, core).start()

    early = ((step_y, -zfirst), (step_z, 5 - zfirst))
    late = early + ((step_x, 8 - zfirst), (step_back_z, 13 - zfirst), (step_back_y, 17 - zfirst))
    z_early = ((z_step_z, ZLAG[0]),)
    z_late = tuple(zip((z_step_y, z_step_x, z_step_back_y, z_step_back_z), ZLAG[1:]))
    sent = 5 - zfirst + pieces

    def step(t, stages, z_stages):
        for stage, lag in stages:
            p = t - lag

            @pl.when((p >= zfirst) & (p < pieces))
            def _():
                stage(p)

        if zfirst > 0:
            for stage, lag in z_stages:
                p = t - lag

                @pl.when((p >= 0) & (p < zfirst))
                def _():
                    stage(p)

    def give_row(r):
        for d in (2, 3, 1):
            give(d, r).start()

    slope_edges()

    @pl.loop(0, own // 2)
    def _(pair):
        grad_in(pair)

        @pl.loop(jnp.minimum(2 * pair, EARLY), jnp.minimum(2 * pair + 2, EARLY))
        def _(r):
            give_row(r)

        @pl.loop(2 * pair, 2 * pair + 2)
        def _(t):
            step(t, early, z_early)

    @pl.loop(own, max(late[-1][1] + pieces, ZLAG[-1] + zfirst))
    def _(t):
        r = EARLY + (t - LATE_AT) // LATE_STEP

        @pl.when((t >= LATE_AT) & (lax.rem(t - LATE_AT, LATE_STEP) == 0) & (r < own))
        def _():
            give_row(r)

        step(t, late, z_late)

        @pl.when(t == sent)
        def _():
            ls_x.wait_recv()
            l3[...] = l2[...] + lr2[...]

            @pl.loop(1, n)
            def _(d):
                loss_to_strip(d, s).start()

    def take_loss(d, v):
        i = lax.rem(s + d, n)
        loss_to_strip(d, i).wait_recv()
        return v + lr3[i]

    loss_ref[...] = lax.fori_loop(1, n, take_loss, l3[...])

    @pl.loop(0, own)
    def _(r):
        for d in range(1, 4):
            give(d, r).wait_send()
            taken(d, r).wait_recv()

    @pl.loop(0, pieces)
    def _(p):
        @pl.when(p >= zfirst)
        def _():
            back_core(p, 1 - core, sy, 0).wait_recv()
            back_core(p, 1 - core, 1 - sy, 1).wait_recv()

        if zfirst > 0:

            @pl.when(p < zfirst)
            def _():
                z_back_core(p, 1 - core).wait_recv()

    @pl.loop(0, last + 1)
    def _(q):
        for d in range(1, 4):
            to = ens_at(d)

            @pl.when(goes(to, q))
            def _():
                row_of(d, to, q, e).wait_send()

    for d in range(4):
        for side in range(2):
            edge_of(side, d, e).wait_send()

    @pl.when(outer)
    def _():
        outer_halo.wait_send()
        outer_edge.wait_send()

    @pl.loop(1, n)
    def _(d):
        loss_to_strip(d, s).wait_send()

    @pl.loop(0, pieces)
    def _(p):
        by_x(p).wait_send()

        @pl.when(p >= zfirst)
        def _():
            by_y(p).wait_send()
            back_y(p, sy).wait_send()
            back_core(p, core, sy, 0).wait_send()
            back_core(p, core, 1 - sy, 1).wait_send()

            @pl.loop(1, nz)
            def _(d):
                by_z(p, d, sz).wait_send()
                back_z(p, d, sz).wait_send()

        if zfirst > 0:

            @pl.when(p < zfirst)
            def _():
                z_by_y(p, 1 - sy).wait_send()
                z_back_y(p, sy).wait_send()
                z_back_core(p, core).wait_send()

                @pl.loop(1, nz)
                def _(d):
                    z_by_z(p, d, sz).wait_send()
                    z_back_z(p, d, sz).wait_send()

    @pl.loop(0, TAPS)
    def _(tap):
        by_core(tap).wait_send()

    for c in edges + [hand, inner_halo, hand_edge, ls_core, ls_x]:
        c.wait_send()


def finish(scale, loss_scale, gi_ref, gk_ref, l_ref, gi_out, gk_out, loss_out, wide, sem):
    taps = wide.shape[0]
    out_gi = pltpu.make_async_copy(gi_ref, gi_out, sem.at[taps])
    out_gi.start()

    def out_tap(tap):
        return pltpu.make_async_copy(wide.at[tap], gk_out.at[tap], sem.at[tap])

    for tap in range(taps):
        for h in range(2):
            v = gk_ref[h, tap * 128 : tap * 128 + 128].astype(F32)
            wide[tap, h * 128 : h * 128 + 128] = v * scale
        out_tap(tap).start()
    loss_out[0, 0] = jnp.sum(l_ref[...]) * loss_scale
    for tap in range(taps):
        out_tap(tap).wait()
    out_gi.wait()


def local(n, latents, targets, kernel):
    mdev, rows, cols, chans = latents.shape
    members = mdev * 4
    own = rows // 4
    slots = own + 2
    cells = members * cols
    pieces, part = pieces_of(n)
    nz = n // 2
    hp = pieces * part * n
    vmem, dma = pltpu.VMEM, pltpu.SemaphoreType.DMA
    hbm = pl.BlockSpec(memory_space=pltpu.HBM)
    on_chip = pl.BlockSpec(memory_space=vmem)
    shifted = vmem((3, slots, members, cols, chans), BF16)
    edge = vmem((2, own, members, chans), F32)
    tile = vmem((8, 128), F32)
    edge_rows = -(-((rows - own) * mdev + 32) // 16) * 16
    gi, gk, loss = pl.pallas_call(
        functools.partial(body, n, members),
        name="crps_step",
        out_shape=(
            vmem(latents.shape, BF16),
            vmem((2, hp, chans), BF16),
            vmem((8, 128), F32),
        ),
        in_specs=[hbm] * 3,
        out_specs=(on_chip,) * 3,
        scratch_shapes=[
            shifted,
            vmem((mdev, rows, cols, chans), BF16),
            vmem((own, cols, chans), BF16),
            vmem((TAPS, chans, chans), BF16),
            vmem((2, edge_rows, chans), F32),
            vmem((2, edge_rows, chans), BF16),
            vmem((2, 4, 32, chans), BF16),
            vmem((2, 4, 32, chans), F32),
            vmem((members, cols, chans), F32),
            shifted,
            vmem((2, TAPS, chans, 128), F32),
            edge,
            vmem((2, own * members, chans), BF16),
            vmem((2, own * members, chans), BF16),
            edge,
            vmem((2, 2, members, chans), F32),
            vmem((members, own, cols, chans), BF16),
            vmem((16, chans), F32),
            vmem((chans, (BLOCKS[0][1] - BLOCKS[0][0]) * cells), BF16),
            vmem((TAPS, chans, 128), F32),
            vmem((hp, chans), F32),
            vmem((hp, chans), BF16),
            vmem((hp, chans), BF16),
            vmem((hp // 2, chans), BF16),
            vmem((nz, pieces * part, chans), BF16),
            vmem((nz, max(first_by_z(n), 1) * 2 * part, chans), BF16),
            vmem((pieces * part, chans), BF16),
            vmem((pieces * part, chans), BF16),
            tile, tile, tile, tile, tile,
            vmem((n, 8, 128), F32),
            dma((3,)), dma((mdev + 2,)),
            dma((4, slots)), dma((4, slots)), dma((1,)), dma((1,)),
            dma((2, 4)), dma((2, 4)), dma((2,)), dma((2,)), dma((4,)), dma((4,)),
            dma((4, own)), dma((4, own)),
            dma((TAPS,)), dma((TAPS,)), dma((pieces,)), dma((pieces,)),
            dma((pieces, nz)), dma((pieces, nz)), dma((pieces,)), dma((pieces,)),
            dma((pieces, nz)), dma((pieces, nz)), dma((pieces,)), dma((pieces,)),
            dma((pieces, 2)), dma((pieces, 2)),
            dma((2,)), dma((2,)), dma((n,)), dma((n,)),
        ],
        compiler_params=pltpu.CompilerParams(
            collective_id=0, has_side_effects=True, vmem_limit_bytes=56 * 2**20
        ),
    )(latents, targets, kernel.reshape(TAPS, chans, chans))
    longitude = cols * n
    gi, gk, loss = pl.pallas_call(
        functools.partial(
            finish, 1.0 / (members * rows * longitude), 1.0 / (rows * longitude * chans)
        ),
        name="finish",
        out_shape=(
            jax.ShapeDtypeStruct(latents.shape, BF16),
            jax.ShapeDtypeStruct((TAPS, chans, chans), F32),
            jax.ShapeDtypeStruct((1, 1), F32),
        ),
        in_specs=[on_chip] * 3,
        out_specs=(hbm, hbm, pl.BlockSpec(memory_space=pltpu.SMEM)),
        scratch_shapes=[vmem((TAPS, chans, chans), F32), dma((TAPS + 1,))],
        compiler_params=pltpu.CompilerParams(vmem_limit_bytes=24 * 2**20),
    )(gi, gk, loss)
    return loss.reshape(()), gi, gk.reshape(3, 3, chans, chans)


def solution(mesh):
    in_specs = (P("ens", None, "space", None), P(None, "space", None), P())
    out_specs = (P(), P("ens", None, "space", None), P())
    return jax.shard_map(
        functools.partial(local, mesh.shape["space"]),
        mesh=mesh, in_specs=in_specs, out_specs=out_specs, check_vma=False,
    )
```

```python
import functools

import jax
import jax.numpy as jnp
from jax import lax
from jax.experimental import pallas as pl
from jax.experimental.pallas import tpu as pltpu
from jax.sharding import PartitionSpec as P

smoothing = 0.1
F32, BF16 = jnp.float32, jnp.bfloat16
NT = (((1,), (1,)), ((), ()))
TAPS = 9
EARLY, LATE_AT, LATE_STEP = 2, 11, 1
BLOCKS = ((0, 4), (4, 8))
ZFIRST = 3
ZLAG = (3, 8, 11, 15, 18)
GROUPS = ((0, 1, 2, 3, 4), (5, 6, 7, 8))


def pieces_of(n):
    units = -(-TAPS * 128 // (16 * n))
    pieces = min(TAPS, units)
    return pieces, 16 * -(-units // pieces)


def first_by_z(n):
    return ZFIRST if pieces_of(n)[0] == TAPS else 0


def body(
    n, members,
    lat_hbm, t_hbm, k_hbm,
    gi_ref, gk_ref, loss_ref,
    x_ref, latv, tv, kv, lef32, leo, lei, lef, fld, sp, acc, eo, eb, eib, ei, eh, gib, lacc, slt,
    r1, g, b2, r2, b3, r3, rz, b4, r4, l1, lr1, l2, lr2, l3, lr3,
    s_in, s_own, s_x, r_x, s_f, r_f, s_le, r_le, s_e, r_e, s_h, r_h, s_g, r_g,
    s_c, r_c, s_y, r_y, s_z, r_z, s_v, r_v, s_az, r_az, s_ay, r_ay, s_ac, r_ac,
    s_ls, r_ls, s_lp, r_lp,
):
    mdev, rows, cols, chans = lat_hbm.shape
    own = rows // 4
    last = own + 1
    cells = members * cols
    pieces, part = pieces_of(n)
    nz = n // 2
    zfirst = first_by_z(n)
    half = part * nz
    span = 2 * half
    e = lax.axis_index("ens")
    s = lax.axis_index("space")
    core = lax.rem(e, 2)
    xx = e // 2
    sy = lax.rem(s, 2)
    sz = s // 2
    outer = xx != core
    cpeer = {"ens": xx * 2 + (1 - core)}
    xpeer = {"ens": (1 - xx) * 2 + core}
    across = {"ens": 3 - e}
    ypeer = {"space": sz * 2 + (1 - sy)}
    right_s = lax.rem(s + 1, n)
    left_s = lax.rem(s + n - 1, n)
    MESH = pl.DeviceIdType.MESH

    def rcopy(src, dst, ss, rs, dev):
        return pltpu.make_async_remote_copy(
            src_ref=src, dst_ref=dst, send_sem=ss, recv_sem=rs,
            device_id=dev, device_id_type=MESH,
        )

    def ens_at(d):
        return lax.rem(e + d, 4)

    def slot_of(c, q):
        return jnp.where(c == 0, last - q, q)

    def base_of(pair):
        return jnp.where(core == 0, own - 2 - 2 * pair, 2 * pair)

    in_lat = pltpu.make_async_copy(lat_hbm, latv, s_in.at[0])
    in_k = pltpu.make_async_copy(k_hbm, kv, s_in.at[1])
    in_t = pltpu.make_async_copy(t_hbm.at[pl.ds(e * own, own)], tv, s_in.at[2])
    in_lat.start()
    in_k.start()
    in_t.start()
    barrier = pltpu.get_barrier_semaphore()
    for d in range(1, 4):
        for strip in (s, right_s, left_s):
            pl.semaphore_signal(
                barrier, inc=1, device_id={"ens": ens_at(d), "space": strip}, device_id_type=MESH
            )

    @pl.loop(1, n)
    def _(d):
        pl.semaphore_signal(
            barrier, inc=1, device_id={"space": lax.rem(s + d, n)}, device_id_type=MESH
        )

    def own_copy(k):
        if k < mdev:
            return pltpu.make_async_copy(
                lat_hbm.at[k, pl.ds(e * own, own)], x_ref.at[1, pl.ds(1, own), e * mdev + k],
                s_own.at[k],
            )
        slot = slot_of(core, 0 if k == mdev else last)
        row = jnp.clip(e * own - 1 + slot, 0, rows - 1)
        return pltpu.make_async_copy(
            lat_hbm.at[:, row], x_ref.at[1, slot, pl.ds(e * mdev, mdev)], s_own.at[k]
        )

    for k in range(mdev + 1):
        own_copy(k).start()

    @pl.when(outer)
    def _():
        own_copy(mdev + 1).start()

    pl.semaphore_wait(barrier, n - 1 + 9)

    def row_of(d, to, q, src):
        slot = slot_of(lax.rem(to, 2), q)
        row = jnp.clip(to * own - 1 + slot, 0, rows - 1)
        return rcopy(
            lat_hbm.at[:, row], x_ref.at[1, slot, pl.ds(mdev * src, mdev)],
            s_x.at[d, q], r_x.at[src, q], {"ens": to},
        )

    def goes(to, q):
        there = (to // 2) != xx
        exists = (q < last) | ((to // 2) != lax.rem(to, 2))
        return exists & ((q > 0) | jnp.logical_not(there))

    def edge_of(side, d, src):
        to = ens_at(d)
        return rcopy(
            leo.at[side, pl.ds(pl.multiple_of(to * own * mdev, 16), 32)], lei.at[1 - side, src],
            s_le.at[side, d], r_le.at[1 - side, src],
            {"ens": to, "space": left_s if side == 0 else right_s},
        )

    def send_rows(first, stop):
        @pl.loop(first, stop)
        def _(j):
            q = jnp.where(j < 3, lax.rem(j + 1, 3), j)
            for d in (2, 3, 1):
                to = ens_at(d)

                @pl.when(goes(to, q))
                def _():
                    row_of(d, to, q, e).start()

    send_rows(0, 1)
    lef32[...] = jnp.zeros_like(lef32)
    in_lat.wait()

    @pl.loop(0, rows)
    def _(row):
        for m in range(mdev):
            v = latv[m, row, 0:16].astype(F32)
            w = latv[m, row, cols - 16 : cols].astype(F32)
            lef32[0, pl.ds((1 + row) * mdev + m, 1)] = v[0:1]
            lef32[1, pl.ds((1 + row) * mdev + m, 1)] = w[15:16]

    leo[...] = lef32[...].astype(BF16)
    for d in (2, 3, 1, 0):
        for side in range(2):
            edge_of(side, d, e).start()
    send_rows(1, last + 1)

    @pl.when(jnp.logical_not(outer))
    def _():
        blank = jnp.zeros((members, cols, chans), BF16)
        slot = slot_of(core, last)
        x_ref[1, slot] = blank
        for c in range(3):
            sp[c, slot] = blank

    hand_slot = slot_of(core, 1)
    get_slot = slot_of(core, 0)
    theirs = pl.ds(2 * mdev * (1 - xx), 2 * mdev)
    hand = rcopy(
        x_ref.at[1, hand_slot, theirs], x_ref.at[1, last - get_slot, theirs],
        s_f.at[0], r_f.at[0], cpeer,
    )

    acc[...] = jnp.zeros_like(acc)
    lacc[...] = jnp.zeros_like(lacc)
    if pieces * span > TAPS * 128:
        tail = pl.ds(TAPS * 128, pieces * span - TAPS * 128)
        g[tail] = jnp.zeros((pieces * span - TAPS * 128, chans), F32)
        b2[tail] = jnp.zeros((pieces * span - TAPS * 128, chans), BF16)
    in_k.wait()
    in_t.wait()
    for k in range(mdev + 1):
        own_copy(k).wait()

    @pl.when(outer)
    def _():
        own_copy(mdev + 1).wait()

    for d in (0, 1, 2, 3):
        for side in range(2):
            edge_of(side, d, ens_at(d)).wait_recv()
    lef[...] = lei[...].astype(F32)

    col = lax.broadcasted_iota(jnp.int32, (cols, chans), 0)

    def shift(ref, slot, edge):
        for mem in range(members):
            v = ref[1, slot, mem].astype(F32)
            lo = jnp.where(col == 0, edge(0, mem), pltpu.roll(v, 1, 0))
            hi = jnp.where(col == cols - 1, edge(1, mem), pltpu.roll(v, cols - 1, 0))
            ref[0, slot, mem] = lo.astype(BF16)
            ref[2, slot, mem] = hi.astype(BF16)

    def ready(q):
        for d in range(1, 4):
            src = ens_at(d)
            there = (src // 2) != xx
            exists = ((q < last) | outer) & ((q > 0) | jnp.logical_not(there))

            @pl.when(exists)
            def _():
                row_of(d, e, q, src).wait_recv()

        @pl.when(q == 0)
        def _():
            hand.wait_recv()

        @pl.when(q == 1)
        def _():
            hand.start()

        slot = slot_of(core, q)
        shift(
            x_ref, slot,
            lambda side, mem: lef[side, mem // mdev, pl.ds(slot * mdev + mem % mdev, 1)],
        )

    def smooth(gap):
        square = gap * gap + smoothing * smoothing
        inv = lax.rsqrt(square)
        return gap * inv, square * inv

    def fields_of(i):
        total = None
        for a in range(3):
            for b in range(3):
                w = x_ref[b, i + a].reshape(cells, chans)
                term = jnp.dot(w, kv[a * 3 + b], preferred_element_type=F32)
                total = term if total is None else total + term
        fld[...] = total.reshape(members, cols, chans)

    def pairs_of(i):
        for blk in range(cols // 16):
            for lane in range(chans // 128):
                ln = pl.ds(lane * 128, 128)
                at = pl.ds(blk * 16, 16)
                tgt = tv[i, at, ln].astype(F32)
                f = [fld[m, at, ln] for m in range(members)]
                sums = [None] * members
                pair_w = None
                for m in range(members):
                    for o in range(m + 1, members):
                        sl, w = smooth(f[m] - f[o])
                        sums[m] = sl if sums[m] is None else sums[m] + sl
                        sums[o] = -sl if sums[o] is None else sums[o] - sl
                        pair_w = w if pair_w is None else pair_w + w
                own_w = None
                for m in range(members):
                    own_s, w = smooth(f[m] - tgt)
                    own_w = w if own_w is None else own_w + w
                    sl = own_s * (1.0 / members) - sums[m] * (1.0 / (members * (members - 1)))
                    sp[1, 1 + i, m, at, ln] = sl.astype(BF16)
                    if blk == 0:
                        eo[0, i, m : m + 1, ln] = sl[0:1]
                    if blk == cols // 16 - 1:
                        eo[1, i, m : m + 1, ln] = sl[15:16]
                lacc[:, ln] += own_w * (1.0 / members) - pair_w * (
                    1.0 / (members * (members - 1))
                )

    def rows_at(p, h, first=0, count=None):
        start = p * span + h * half + first
        return pl.ds(pl.multiple_of(start, 16), half if count is None else count)

    def by_core(tap):
        return rcopy(acc.at[1 - core, tap], r1.at[tap], s_c.at[tap], r_c.at[tap], cpeer)

    def by_y(p):
        there = rows_at(p, 1 - sy)
        return rcopy(b2.at[there], r2.at[there], s_y.at[p], r_y.at[p], ypeer)

    def y_here(p):
        here = rows_at(p, sy)
        return rcopy(b2.at[here], r2.at[here], s_y.at[p], r_y.at[p], ypeer)

    def z_rows(p, j, h=None):
        start = p * span + j * 2 * part + (0 if h is None else h * part)
        return pl.ds(pl.multiple_of(start, 16), 2 * part if h is None else part)

    def z_by_z(p, d, src):
        to = lax.rem(sz + d, nz)
        return rcopy(
            b2.at[z_rows(p, to)], rz.at[src, pl.ds(pl.multiple_of(p * 2 * part, 16), 2 * part)],
            s_z.at[p, d], r_z.at[p, src], {"space": to * 2 + sy},
        )

    def z_by_y(p, h):
        at = z_rows(p, sz, h)
        return rcopy(b2.at[at], r2.at[at], s_y.at[p], r_y.at[p], ypeer)

    def z_back_y(p, h):
        mine = gk_ref.at[core, z_rows(p, sz, h)]
        return rcopy(mine, mine, s_ay.at[p], r_ay.at[p], ypeer)

    def z_back_z(p, d, src):
        mine = gk_ref.at[core, z_rows(p, src)]
        to = lax.rem(sz + d, nz)
        return rcopy(mine, mine, s_az.at[p, d], r_az.at[p, src], {"space": to * 2 + sy})

    def z_back_core(p, c):
        mine = gk_ref.at[c, pl.ds(pl.multiple_of(p * span, 16), span)]
        return rcopy(mine, mine, s_ac.at[p, 0], r_ac.at[p, 0], cpeer)

    def core_sums():
        @pl.loop(0, TAPS)
        def _(tap):
            by_core(tap).wait_recv()
            v = (acc[core, tap] + r1[tap]).T
            at = pl.ds(pl.multiple_of(tap * 128, 128), 128)
            g[at] = v
            b2[at] = v.astype(BF16)
            ready_pieces = jnp.where(tap == TAPS - 1, pieces, (tap + 1) * 128 // span)

            @pl.when(ready_pieces > tap * 128 // span)
            def _():
                p = ready_pieces - 1

                @pl.when(p >= zfirst)
                def _():
                    by_y(p).start()

                if zfirst > 0:

                    @pl.when(p < zfirst)
                    def _():
                        @pl.loop(1, nz)
                        def _(d):
                            z_by_z(p, d, sz).start()


    def kernel_terms(start, stop, final):
        count = BLOCKS[0][1] - BLOCKS[0][0]
        i = jnp.where(core == 0, own - stop, start)

        for group, taps in enumerate(GROUPS):

            @pl.loop(0, count // 2)
            def _(k):
                at = pl.ds(pl.multiple_of(k * 2 * cells, 128), 2 * cells)
                if group == 0:
                    v = sp[1, pl.ds(1 + i + 2 * k, 2)].reshape(2 * cells, chans).astype(F32)
                    v = v.T.astype(BF16)
                    slt[:, at] = v
                else:
                    v = slt[:, at]
                for tap in taps:
                    a, b = tap // 3, tap % 3
                    w = x_ref[b, pl.ds(i + 2 * k + a, 2)].reshape(2 * cells, chans)
                    p = jnp.dot(v, w, preferred_element_type=F32)
                    for h in range(2):
                        acc[h, tap] += p[:, h * 128 : h * 128 + 128]

            @pl.when(final)
            def _():
                @pl.loop(taps[0], taps[-1] + 1)
                def _(tap):
                    by_core(tap).start()

    inner_halo = rcopy(
        sp.at[1, hand_slot], sp.at[1, last - get_slot], s_h.at[0], r_h.at[0], cpeer
    )
    outer_slot = slot_of(core, own)
    outer_halo = rcopy(
        sp.at[1, outer_slot], sp.at[1, last - slot_of(core, last)], s_h.at[1], r_h.at[1], across
    )
    edges = [
        rcopy(eb.at[1], eib.at[0], s_e.at[0], r_e.at[0], {"space": right_s}),
        rcopy(eb.at[0], eib.at[1], s_e.at[1], r_e.at[1], {"space": left_s}),
    ]

    @pl.loop(0, len(BLOCKS))
    def _(blk):
        start = jnp.int32(BLOCKS[0][0])
        stop = jnp.int32(BLOCKS[0][1])
        for k in range(1, len(BLOCKS)):
            start = jnp.where(blk == k, BLOCKS[k][0], start)
            stop = jnp.where(blk == k, BLOCKS[k][1], stop)
        first = jnp.where(blk == 0, 0, start + 2)

        @pl.loop(first, stop + 2)
        def _(t):
            ready(jnp.where(t < 3, lax.rem(t + 1, 3), t))

            @pl.when(t >= 2)
            def _():
                i = slot_of(core, t - 1) - 1
                fields_of(i)
                pairs_of(i)

            @pl.when(t == 2)
            def _():
                inner_halo.start()

            @pl.when(t == last)
            def _():
                eb[...] = eo[...].reshape(eb.shape).astype(BF16)
                for c in edges:
                    c.start()

                @pl.when(outer)
                def _():
                    outer_halo.start()

        kernel_terms(start, stop, blk == len(BLOCKS) - 1)

    core_sums()
    total = lacc[...]
    total = total[0:8, 0:128] + total[8:16, 0:128] + total[0:8, 128:256] + total[8:16, 128:256]
    l1[...] = total
    ls_core = rcopy(l1, lr1, s_ls.at[0], r_ls.at[0], cpeer)
    ls_core.start()
    ls_core.wait_recv()
    l2[...] = l1[...] + lr1[...]
    ls_x = rcopy(l2, lr2, s_ls.at[1], r_ls.at[1], xpeer)
    ls_x.start()

    hand_edge = rcopy(ei.at[:, hand_slot - 1], eh.at[0], s_h.at[2], r_h.at[2], cpeer)
    outer_edge = rcopy(ei.at[:, outer_slot - 1], eh.at[1], s_h.at[3], r_h.at[3], across)

    def slope_edges():
        for c in edges:
            c.wait_recv()
        ei[...] = eib[...].astype(F32).reshape(ei.shape)
        hand_edge.start()

        @pl.when(outer)
        def _():
            outer_edge.start()

        @pl.loop(0, own)
        def _(i):
            shift(sp, 1 + i, lambda side, mem: ei[side, i, mem : mem + 1])

        inner_halo.wait_recv()
        hand_edge.wait_recv()

    def by_z(p, d, src):
        to = lax.rem(sz + d, nz)
        return rcopy(
            b3.at[pl.ds(pl.multiple_of((p * nz + to) * part, 16), part)],
            r3.at[src, pl.ds(pl.multiple_of(p * part, 16), part)],
            s_z.at[p, d], r_z.at[p, src], {"space": to * 2 + sy},
        )

    def row_at(c, r):
        return jnp.where(c == 0, own - 2 - 2 * (r // 2), 2 * (r // 2)) + lax.rem(r, 2)

    def give(d, r):
        to, i = ens_at(d), row_at(core, r)
        return rcopy(
            gib.at[pl.ds(to * mdev, mdev), i], gi_ref.at[:, e * own + i],
            s_g.at[d, r], r_g.at[e, r], {"ens": to},
        )

    def taken(d, r):
        src = ens_at(d)
        i = row_at(lax.rem(src, 2), r)
        return rcopy(
            gib.at[pl.ds(e * mdev, mdev), i], gi_ref.at[:, src * own + i],
            s_g.at[d, r], r_g.at[src, r], {"ens": e},
        )

    def grad_in(pair):
        @pl.when((pair == 0) | ((pair == own // 2 - 1) & outer))
        def _():
            @pl.when(pair > 0)
            def _():
                outer_halo.wait_recv()
                outer_edge.wait_recv()

            k = jnp.where(pair == 0, 0, 1)
            shift(
                sp, slot_of(core, jnp.where(pair == 0, 0, last)),
                lambda side, mem: eh[k, side, mem : mem + 1],
            )

        i = base_of(pair)
        total = None
        for a in range(3):
            for b in range(3):
                w = sp[2 - b, pl.ds(i + 2 - a, 2)].reshape(2 * cells, chans)
                term = lax.dot_general(w, kv[a * 3 + b], NT, preferred_element_type=F32)
                total = term if total is None else total + term
        total = total.reshape(2, members, cols, chans).astype(BF16)
        for r in range(2):
            gib[:, i + r] = total[r]
        for m in range(mdev):
            gi_ref[m, pl.ds(e * own + i, 2)] = gib[e * mdev + m, pl.ds(i, 2)]

    def loss_to_strip(d, i):
        return rcopy(l3, lr3.at[i], s_lp.at[d], r_lp.at[i], {"space": lax.rem(s + d, n)})

    def by_x(p):
        at = pl.ds(pl.multiple_of(p * part, 16), part)
        return rcopy(b4.at[at], r4.at[at], s_v.at[p], r_v.at[p], xpeer)

    def back_z(p, d, src):
        mine = gk_ref.at[core, rows_at(p, sy, src * part, part)]
        to = lax.rem(sz + d, nz)
        return rcopy(mine, mine, s_az.at[p, d], r_az.at[p, src], {"space": to * 2 + sy})

    def back_y(p, h):
        mine = gk_ref.at[core, rows_at(p, h)]
        return rcopy(mine, mine, s_ay.at[p], r_ay.at[p], ypeer)

    def back_core(p, c, h, k):
        mine = gk_ref.at[c, rows_at(p, h)]
        return rcopy(mine, mine, s_ac.at[p, k], r_ac.at[p, k], cpeer)

    def step_y(p):
        y_here(p).wait_recv()
        here = rows_at(p, sy)
        total = g[here] + r2[here].astype(F32)
        g[here] = total
        b3[pl.ds(pl.multiple_of(p * half, 16), half)] = total.astype(BF16)

        @pl.loop(1, nz)
        def _(d):
            by_z(p, d, sz).start()

    def step_z(p):
        def take(d, v):
            src = lax.rem(sz + d, nz)
            by_z(p, d, src).wait_recv()
            return v + r3[src, pl.ds(pl.multiple_of(p * part, 16), part)].astype(F32)

        v = lax.fori_loop(1, nz, take, g[rows_at(p, sy, sz * part, part)])
        b4[pl.ds(pl.multiple_of(p * part, 16), part)] = v.astype(BF16)
        by_x(p).start()

    def step_x(p):
        by_x(p).wait_recv()
        at = pl.ds(pl.multiple_of(p * part, 16), part)
        v = b4[at].astype(F32) + r4[at].astype(F32)
        gk_ref[core, rows_at(p, sy, sz * part, part)] = v.astype(BF16)

        @pl.loop(1, nz)
        def _(d):
            back_z(p, d, sz).start()

    def step_back_z(p):
        @pl.loop(1, nz)
        def _(d):
            back_z(p, d, lax.rem(sz + d, nz)).wait_recv()

        back_y(p, sy).start()
        back_core(p, core, sy, 0).start()

    def step_back_y(p):
        back_y(p, 1 - sy).wait_recv()
        back_core(p, core, 1 - sy, 1).start()

    def z_step_z(p):
        at = z_rows(p, sz)

        def take(d, v):
            src = lax.rem(sz + d, nz)
            z_by_z(p, d, src).wait_recv()
            return v + rz[src, pl.ds(pl.multiple_of(p * 2 * part, 16), 2 * part)].astype(F32)

        v = lax.fori_loop(1, nz, take, g[at])
        g[at] = v
        b2[at] = v.astype(BF16)
        z_by_y(p, 1 - sy).start()

    def z_step_y(p):
        z_by_y(p, sy).wait_recv()
        at = z_rows(p, sz, sy)
        v = g[at] + r2[at].astype(F32)
        b4[pl.ds(pl.multiple_of(p * part, 16), part)] = v.astype(BF16)
        by_x(p).start()

    def z_step_x(p):
        by_x(p).wait_recv()
        at = pl.ds(pl.multiple_of(p * part, 16), part)
        v = b4[at].astype(F32) + r4[at].astype(F32)
        gk_ref[core, z_rows(p, sz, sy)] = v.astype(BF16)
        z_back_y(p, sy).start()

    def z_step_back_y(p):
        z_back_y(p, 1 - sy).wait_recv()

        @pl.loop(1, nz)
        def _(d):
            z_back_z(p, d, sz).start()

    def z_step_back_z(p):
        @pl.loop(1, nz)
        def _(d):
            z_back_z(p, d, lax.rem(sz + d, nz)).wait_recv()

        z_back_core(p, core).start()

    early = ((step_y, -zfirst), (step_z, 5 - zfirst))
    late = early + ((step_x, 8 - zfirst), (step_back_z, 13 - zfirst), (step_back_y, 17 - zfirst))
    z_early = ((z_step_z, ZLAG[0]),)
    z_late = tuple(zip((z_step_y, z_step_x, z_step_back_y, z_step_back_z), ZLAG[1:]))
    sent = 5 - zfirst + pieces

    def step(t, stages, z_stages):
        for stage, lag in stages:
            p = t - lag

            @pl.when((p >= zfirst) & (p < pieces))
            def _():
                stage(p)

        if zfirst > 0:
            for stage, lag in z_stages:
                p = t - lag

                @pl.when((p >= 0) & (p < zfirst))
                def _():
                    stage(p)

    def give_row(r):
        for d in (2, 3, 1):
            give(d, r).start()

    slope_edges()

    @pl.loop(0, own // 2)
    def _(pair):
        grad_in(pair)

        @pl.loop(jnp.minimum(2 * pair, EARLY), jnp.minimum(2 * pair + 2, EARLY))
        def _(r):
            give_row(r)

        @pl.loop(2 * pair, 2 * pair + 2)
        def _(t):
            step(t, early, z_early)

    @pl.loop(own, max(late[-1][1] + pieces, ZLAG[-1] + zfirst))
    def _(t):
        r = EARLY + (t - LATE_AT) // LATE_STEP

        @pl.when((t >= LATE_AT) & (lax.rem(t - LATE_AT, LATE_STEP) == 0) & (r < own))
        def _():
            give_row(r)

        step(t, late, z_late)

        @pl.when(t == sent)
        def _():
            ls_x.wait_recv()
            l3[...] = l2[...] + lr2[...]

            @pl.loop(1, n)
            def _(d):
                loss_to_strip(d, s).start()

    def take_loss(d, v):
        i = lax.rem(s + d, n)
        loss_to_strip(d, i).wait_recv()
        return v + lr3[i]

    loss_ref[...] = lax.fori_loop(1, n, take_loss, l3[...])

    @pl.loop(0, own)
    def _(r):
        for d in range(1, 4):
            give(d, r).wait_send()
            taken(d, r).wait_recv()

    @pl.loop(0, pieces)
    def _(p):
        @pl.when(p >= zfirst)
        def _():
            back_core(p, 1 - core, sy, 0).wait_recv()
            back_core(p, 1 - core, 1 - sy, 1).wait_recv()

        if zfirst > 0:

            @pl.when(p < zfirst)
            def _():
                z_back_core(p, 1 - core).wait_recv()

    @pl.loop(0, last + 1)
    def _(q):
        for d in range(1, 4):
            to = ens_at(d)

            @pl.when(goes(to, q))
            def _():
                row_of(d, to, q, e).wait_send()

    for d in range(4):
        for side in range(2):
            edge_of(side, d, e).wait_send()

    @pl.when(outer)
    def _():
        outer_halo.wait_send()
        outer_edge.wait_send()

    @pl.loop(1, n)
    def _(d):
        loss_to_strip(d, s).wait_send()

    @pl.loop(0, pieces)
    def _(p):
        by_x(p).wait_send()

        @pl.when(p >= zfirst)
        def _():
            by_y(p).wait_send()
            back_y(p, sy).wait_send()
            back_core(p, core, sy, 0).wait_send()
            back_core(p, core, 1 - sy, 1).wait_send()

            @pl.loop(1, nz)
            def _(d):
                by_z(p, d, sz).wait_send()
                back_z(p, d, sz).wait_send()

        if zfirst > 0:

            @pl.when(p < zfirst)
            def _():
                z_by_y(p, 1 - sy).wait_send()
                z_back_y(p, sy).wait_send()
                z_back_core(p, core).wait_send()

                @pl.loop(1, nz)
                def _(d):
                    z_by_z(p, d, sz).wait_send()
                    z_back_z(p, d, sz).wait_send()

    @pl.loop(0, TAPS)
    def _(tap):
        by_core(tap).wait_send()

    for c in edges + [hand, inner_halo, hand_edge, ls_core, ls_x]:
        c.wait_send()


def finish(scale, loss_scale, gi_ref, gk_ref, l_ref, gi_out, gk_out, loss_out, wide, sem):
    taps = wide.shape[0]
    out_gi = pltpu.make_async_copy(gi_ref, gi_out, sem.at[taps])
    out_gi.start()

    def out_tap(tap):
        return pltpu.make_async_copy(wide.at[tap], gk_out.at[tap], sem.at[tap])

    for tap in range(taps):
        for h in range(2):
            v = gk_ref[h, tap * 128 : tap * 128 + 128].astype(F32)
            wide[tap, h * 128 : h * 128 + 128] = v * scale
        out_tap(tap).start()
    loss_out[0, 0] = jnp.sum(l_ref[...]) * loss_scale
    for tap in range(taps):
        out_tap(tap).wait()
    out_gi.wait()


def local(n, latents, targets, kernel):
    mdev, rows, cols, chans = latents.shape
    members = mdev * 4
    own = rows // 4
    slots = own + 2
    cells = members * cols
    pieces, part = pieces_of(n)
    nz = n // 2
    hp = pieces * part * n
    vmem, dma = pltpu.VMEM, pltpu.SemaphoreType.DMA
    hbm = pl.BlockSpec(memory_space=pltpu.HBM)
    on_chip = pl.BlockSpec(memory_space=vmem)
    shifted = vmem((3, slots, members, cols, chans), BF16)
    edge = vmem((2, own, members, chans), F32)
    tile = vmem((8, 128), F32)
    edge_rows = -(-((rows - own) * mdev + 32) // 16) * 16
    gi, gk, loss = pl.pallas_call(
        functools.partial(body, n, members),
        name="crps_step",
        out_shape=(
            vmem(latents.shape, BF16),
            vmem((2, hp, chans), BF16),
            vmem((8, 128), F32),
        ),
        in_specs=[hbm] * 3,
        out_specs=(on_chip,) * 3,
        scratch_shapes=[
            shifted,
            vmem((mdev, rows, cols, chans), BF16),
            vmem((own, cols, chans), BF16),
            vmem((TAPS, chans, chans), BF16),
            vmem((2, edge_rows, chans), F32),
            vmem((2, edge_rows, chans), BF16),
            vmem((2, 4, 32, chans), BF16),
            vmem((2, 4, 32, chans), F32),
            vmem((members, cols, chans), F32),
            shifted,
            vmem((2, TAPS, chans, 128), F32),
            edge,
            vmem((2, own * members, chans), BF16),
            vmem((2, own * members, chans), BF16),
            edge,
            vmem((2, 2, members, chans), F32),
            vmem((members, own, cols, chans), BF16),
            vmem((16, chans), F32),
            vmem((chans, (BLOCKS[0][1] - BLOCKS[0][0]) * cells), BF16),
            vmem((TAPS, chans, 128), F32),
            vmem((hp, chans), F32),
            vmem((hp, chans), BF16),
            vmem((hp, chans), BF16),
            vmem((hp // 2, chans), BF16),
            vmem((nz, pieces * part, chans), BF16),
            vmem((nz, max(first_by_z(n), 1) * 2 * part, chans), BF16),
            vmem((pieces * part, chans), BF16),
            vmem((pieces * part, chans), BF16),
            tile, tile, tile, tile, tile,
            vmem((n, 8, 128), F32),
            dma((3,)), dma((mdev + 2,)),
            dma((4, slots)), dma((4, slots)), dma((1,)), dma((1,)),
            dma((2, 4)), dma((2, 4)), dma((2,)), dma((2,)), dma((4,)), dma((4,)),
            dma((4, own)), dma((4, own)),
            dma((TAPS,)), dma((TAPS,)), dma((pieces,)), dma((pieces,)),
            dma((pieces, nz)), dma((pieces, nz)), dma((pieces,)), dma((pieces,)),
            dma((pieces, nz)), dma((pieces, nz)), dma((pieces,)), dma((pieces,)),
            dma((pieces, 2)), dma((pieces, 2)),
            dma((2,)), dma((2,)), dma((n,)), dma((n,)),
        ],
        compiler_params=pltpu.CompilerParams(
            collective_id=0, has_side_effects=True, vmem_limit_bytes=56 * 2**20
        ),
    )(latents, targets, kernel.reshape(TAPS, chans, chans))
    longitude = cols * n
    gi, gk, loss = pl.pallas_call(
        functools.partial(
            finish, 1.0 / (members * rows * longitude), 1.0 / (rows * longitude * chans)
        ),
        name="finish",
        out_shape=(
            jax.ShapeDtypeStruct(latents.shape, BF16),
            jax.ShapeDtypeStruct((TAPS, chans, chans), F32),
            jax.ShapeDtypeStruct((1, 1), F32),
        ),
        in_specs=[on_chip] * 3,
        out_specs=(hbm, hbm, pl.BlockSpec(memory_space=pltpu.SMEM)),
        scratch_shapes=[vmem((TAPS, chans, chans), F32), dma((TAPS + 1,))],
        compiler_params=pltpu.CompilerParams(vmem_limit_bytes=24 * 2**20),
    )(gi, gk, loss)
    return loss.reshape(()), gi, gk.reshape(3, 3, chans, chans)


def solution(mesh):
    in_specs = (P("ens", None, "space", None), P(None, "space", None), P())
    out_specs = (P(), P("ens", None, "space", None), P())
    return jax.shard_map(
        functools.partial(local, mesh.shape["space"]),
        mesh=mesh, in_specs=in_specs, out_specs=out_specs, check_vma=False,
    )
```
